256 devices in a mesh: segment: 4 (over y), dom: 64 (over z, x, core).
Axes of the slice: x: 4, y: 4, z: 8, core: 2. Of those that a mesh axis runs over, the one named last changes fastest.
Arguments:
- features: bfloat16 [4, 32768, 512], P(None, 'dom'), may hold values from -6 to 6
- layer_weights: bfloat16 [8, 1024, 512], P('segment'), may hold values from -0.1875 to 0.1875
- layer_bias: float32 [8, 512], P('segment'), may hold values from -3 to 3
- layer_gain: float32 [8, 512], P('segment'), may hold values from 0.1 to 1.9
- tile_val: bfloat16 [256, 4, 128, 128], P('dom'), may hold values from -0.25 to 0.25
- tile_col: int32 [256, 4], P('dom'), may hold values from 0 to 3
- tile_count: int32 [256], P('dom'), may hold values from 1 to 4, as said below
- cross_val: bfloat16 [8, 256, 128, 128], P('segment', 'dom'), may hold values from -0.5 to 0.5
- send_rows: int32 [8, 8192], P('segment', 'dom'), may hold values from 0 to 511, as said below
Outputs:
- segment_out: bfloat16 [4, 4, 32768, 512], P('segment', None, 'dom')
The draws below stay inside these ranges and needn't reach their ends.
Inputs may be any that keep to these rules, and one draw needn't show every extreme that they name: `tile_count`: in some row block of the graph all 4 slots are live. `send_rows`: each partition's list at a layer holds 128 distinct local node indices and contains 512 - 1.
All inputs are finite; a program needn't handle non-finite values.
Results may differ from the reference program's by a relative error of at most 0.012.
Values may be sent and summed in bfloat16 or wider, within the bound.
A program may use at most 64 MiB of HBM per device.

```python
import jax
import jax.numpy as jnp
import numpy as np
from jax import lax

D = 512
TILE = 128
SLOTS = 4
LS = 2
BOUND_ROWS = 128
NODES_DEV = 512
MICRO = 4
BLK_DEV = 4
NODES = 32768
NBLK = 256
LAYERS = 8
BOUND = 8192
N_DOM = 64


def draw_tile_count(key, part):
    parts_n = NBLK // BLK_DEV
    key_a = jax.random.fold_in(key, 11)
    key_b = jax.random.fold_in(key, 12)
    key_c = jax.random.fold_in(key, 13)
    key_d = jax.random.fold_in(key, 14)
    level = jax.random.randint(key_a, (parts_n,), 1, SLOTS + 1)
    chosen = jax.random.randint(key_b, (), 0, parts_n)
    level = jnp.where(jnp.arange(parts_n) == chosen, SLOTS, level)
    counts = jax.random.randint(key_c, (parts_n, BLK_DEV), 1, SLOTS + 1)
    counts = jnp.minimum(counts, level[:, None])
    place = jax.random.randint(key_d, (parts_n,), 0, BLK_DEV)
    counts = jnp.where(jnp.arange(BLK_DEV)[None, :] == place[:, None], level[:, None], counts)
    return counts.reshape(NBLK).astype(jnp.int32)


def draw_send_rows(key, part):
    parts_n = BOUND // BOUND_ROWS
    key_a = jax.random.fold_in(key, 21)
    key_b = jax.random.fold_in(key, 22)
    scores = jax.random.randint(key_a, (LAYERS, parts_n, NODES_DEV - 1), 0, 2 ** 16)
    scores = scores * NODES_DEV + jnp.arange(NODES_DEV - 1, dtype=jnp.int32)
    order = jnp.argsort(scores, axis=-1).astype(jnp.int32)
    picked = order[:, :, :BOUND_ROWS - 1]
    last_row = jnp.full((LAYERS, parts_n, 1), NODES_DEV - 1, jnp.int32)
    listed = jnp.concatenate([picked, last_row], axis=-1)
    offset = jax.random.randint(key_b, (LAYERS, parts_n, 1), 0, BOUND_ROWS)
    where_from = (jnp.arange(BOUND_ROWS, dtype=jnp.int32)[None, None, :] + offset) % BOUND_ROWS
    listed = jnp.take_along_axis(listed, where_from, axis=-1)
    return listed.reshape(LAYERS, BOUND).astype(jnp.int32)


def touch_ends(array, key, least, largest):
    longest = array.shape.index(max(array.shape))
    spots = []
    for shift in (0, 1):
        where = [jax.random.randint(jax.random.fold_in(key, axis), (), 0, length) for axis, length in enumerate(array.shape)]
        where[longest] = (where[longest] + shift) % array.shape[longest]
        spots.append(tuple(where))
    return array.at[spots[0]].set(least).at[spots[1]].set(largest)


def steps_of(rng, dims, cuts, low, high):
    def one(axis_at, shards_of):
        draws = jax.random.uniform(jax.random.fold_in(jax.random.fold_in(rng, 6), axis_at), (shards_of,), jnp.float32, low / len(cuts), high / len(cuts))
        return jnp.repeat(jnp.exp(draws), dims[axis_at] // shards_of).reshape((-1,) + (1,) * (len(dims) - axis_at - 1))

    factor_of = one(*cuts[0])
    for cut in cuts[1:]:
        factor_of = factor_of * one(*cut)
    return factor_of


def normal_values(stream_key, shape, scale, reach, pieces=(), kind=jnp.bfloat16):
    drawn = scale * jax.random.normal(stream_key, shape, jnp.float32)
    if pieces:
        drawn = drawn * steps_of(stream_key, shape, pieces, -0.22, 0.18)
    return jnp.clip(drawn, -reach, reach).astype(kind)


def setup_inputs(seed: int = 0) -> dict:
    key_of = jax.random.split(jax.random.key(seed), 10)
    features = normal_values(key_of[0], (MICRO, NODES, D), 1.0, 6.0, ((1, 64),))
    layer_weights = normal_values(key_of[1], (LAYERS, 2 * D, D), (2 * D) ** -0.5, 0.1875, ((0, 4),))
    layer_bias = normal_values(key_of[2], (LAYERS, D), 0.5, 3.0, ((0, 4),), jnp.float32)
    layer_gain = jnp.clip(1.0 + 0.18 * jax.random.normal(key_of[3], (LAYERS, D), jnp.float32), 0.1, 1.9)
    tile_val = normal_values(key_of[4], (NBLK, SLOTS, TILE, TILE), (TILE * SLOTS) ** -0.5, 0.25, ((0, 64),))
    tile_col = touch_ends(jax.random.randint(key_of[5], (NBLK, SLOTS), 0, BLK_DEV), jax.random.fold_in(key_of[5], 1), 0, BLK_DEV - 1).astype(jnp.int32)
    tile_count = draw_tile_count(jax.random.fold_in(key_of[9], 71), 0)
    cross_val = normal_values(key_of[7], (LAYERS, NBLK, TILE, BOUND_ROWS), BOUND_ROWS ** -0.5, 0.5, ((0, 4), (1, 64)))
    send_rows = draw_send_rows(jax.random.fold_in(key_of[9], 71), 0)
    return {"features": features, "layer_weights": layer_weights, "layer_bias": layer_bias, "layer_gain": layer_gain, "tile_val": tile_val, "tile_col": tile_col, "tile_count": tile_count, "cross_val": cross_val, "send_rows": send_rows}


def one_layer(h, layer, layer_weights, layer_bias, layer_gain, tile_val, gidx, tile_count, cross_val, send_rows):
    hf = h.astype(jnp.float32)
    meansq = lax.optimization_barrier(jnp.mean(hf * hf, axis=-1, keepdims=True))
    x = (hf * lax.rsqrt(meansq + 1e-05) * layer_gain[layer]).astype(jnp.bfloat16)
    nbits = N_DOM.bit_length() - 1
    slot_pos = layer % LS
    bit = slot_pos * (nbits - 1) // max(LS - 1, 1)
    partner = np.arange(N_DOM) ^ 1 << bit
    parted = x.reshape(N_DOM, NODES_DEV, D)
    rows = send_rows[layer].reshape(N_DOM, BOUND_ROWS).astype(jnp.int32)
    sent = jnp.take_along_axis(parted, rows[:, :, None], axis=1)
    recv = sent[partner]
    blocks = x.reshape(NBLK, TILE, D)
    acc = jnp.zeros((NBLK, TILE, D), jnp.float32)
    for slot in range(SLOTS):
        source = blocks[gidx[:, slot]].astype(jnp.float32)
        tiles = tile_val[:, slot].astype(jnp.float32)
        live = (slot < tile_count)[:, None, None]
        prod = jnp.einsum('bij,bjd->bid', tiles, source)
        acc = acc + jnp.where(live, prod, jnp.float32(0.0))
    cross = cross_val[layer].reshape(N_DOM, BLK_DEV, TILE, BOUND_ROWS).astype(jnp.float32)
    remote = jnp.einsum('pbir,prd->pbid', cross, recv.astype(jnp.float32))
    acc = acc + remote.reshape(NBLK, TILE, D)
    agg = acc.reshape(NODES, D).astype(jnp.bfloat16)
    z = jnp.dot(x, layer_weights[layer, :D], preferred_element_type=jnp.float32)
    z = z + jnp.dot(agg, layer_weights[layer, D:], preferred_element_type=jnp.float32)
    z = z + layer_bias[layer]
    return (hf + jax.nn.silu(z)).astype(jnp.bfloat16)

def reference(features, layer_weights, layer_bias, layer_gain, tile_val, tile_col, tile_count, cross_val, send_rows):
    base = jnp.arange(NBLK, dtype=jnp.int32) // BLK_DEV * BLK_DEV
    gidx = (base[:, None] + tile_col).astype(jnp.int32)
    per_micro = []
    for micro_id in range(MICRO):
        h = features[micro_id]
        per_segment = []
        for layer in range(LAYERS):
            h = one_layer(h, layer, layer_weights, layer_bias, layer_gain, tile_val, gidx, tile_count, cross_val, send_rows)
            if layer % LS == LS - 1:
                per_segment.append(h)
        per_micro.append(jnp.stack(per_segment))
    return jnp.stack(per_micro, axis=1)
```

```python
import functools

import jax
import jax.numpy as jnp
from jax import lax
from jax.experimental import pallas as pl
from jax.experimental.pallas import tpu as pltpu
from jax.sharding import PartitionSpec as P

LS = 2
X_CHIPS = 4
MESH = pl.DeviceIdType.MESH
F32 = jnp.float32
BF16 = jnp.bfloat16


def dot(a, b):
    return jnp.dot(a, b, preferred_element_type=F32)


def body(
    nseg,
    ndom,
    xc,
    feat,
    wts,
    bias,
    gain,
    tiles_hbm,
    cols,
    counts,
    cross_hbm,
    rows,
    out,
    wbuf,
    cbuf,
    small,
    hsec,
    hmid,
    xb,
    adj,
    tiles,
    snd,
    rcv,
    zp,
    loc_sem,
    ex_send,
    ex_recv,
    y_send,
    y_recv,
    c_send,
    c_recv,
    s_send,
    s_recv,
    x_send,
    x_recv,
    sib_send,
    sib_recv,
    o_send,
    o_recv,
    o_loc,
):
    s = lax.axis_index("segment")
    d = lax.axis_index("dom")
    core = d % 2
    xi = (d // 2) % xc
    base = d - (d % (2 * xc))
    sib = base + xi * 2 + (1 - core)
    anti = (d + ndom // 2) % ndom
    depth, width = wbuf.shape[1], wbuf.shape[2]
    nblk, nslot, tile = tiles_hbm.shape[0], tiles_hbm.shape[1], tiles_hbm.shape[2]
    nodes = nblk * tile
    bound = rows.shape[1]
    shard = depth // (2 * xc)
    mine = (xi * 2 + core) * shard

    def yid(dy):
        return ((s + dy) % nseg, d)

    def xid(dx):
        return (s, base + ((xi + dx) % xc) * 2 + core)

    load_h = pltpu.make_async_copy(feat.at[s], hsec.at[0], loc_sem.at[0])
    load_w = pltpu.make_async_copy(wts, wbuf.at[pl.ds(s * LS, LS)], loc_sem.at[1])
    load_c = pltpu.make_async_copy(cross_hbm, cbuf.at[pl.ds(s * LS, LS)], loc_sem.at[2])
    load_t = pltpu.make_async_copy(tiles_hbm, tiles, loc_sem.at[3])
    load_t.start()
    load_h.start()
    load_w.start()
    load_c.start()

    for i in range(LS):
        small[s * LS + i] = jnp.zeros((8, width), F32)
        small[s * LS + i, 0:1, :] = bias[i : i + 1, :]
        small[s * LS + i, 1:2, :] = gain[i : i + 1, :]
        small[s * LS + i, 2:3, 0:bound] = rows[i : i + 1, :].astype(F32)

    barrier = pltpu.get_barrier_semaphore()
    peers = [yid(dy) for dy in range(1, nseg)]
    peers += [xid(dx) for dx in range(1, xc)]
    peers += [(s, sib), (s, anti)]
    for peer in peers:
        pl.semaphore_signal(barrier, inc=1, device_id=peer, device_id_type=MESH)
    pl.semaphore_wait(barrier, len(peers))

    def remote(src, dst, send, recv, peer):
        return pltpu.make_async_remote_copy(
            src_ref=src,
            dst_ref=dst,
            send_sem=send,
            recv_sem=recv,
            device_id=peer,
            device_id_type=MESH,
        )

    def w_copy(i, l, dy):
        return remote(
            wts.at[i, pl.ds(mine, shard)],
            wbuf.at[l, pl.ds(mine, shard)],
            y_send.at[i, dy],
            y_recv.at[l],
            yid(dy),
        )

    def c_copy(i, l, dy):
        return remote(cross_hbm.at[i], cbuf.at[l], c_send.at[i, dy], c_recv.at[l], yid(dy))

    def s_copy(k, dy):
        part = small.at[pl.ds(k * LS, LS)]
        return remote(part, part, s_send.at[dy], s_recv.at[k], yid(dy))

    def x_copy(l, dx):
        part = wbuf.at[l, pl.ds(mine, shard)]
        return remote(part, part, x_send.at[l, dx], x_recv.at[l, dx], xid(dx))

    def x_from(l, dx):
        start = (((xi + xc - dx) % xc) * 2 + core) * shard
        return wbuf.at[l, pl.ds(start, shard)]

    def sib_copy(l, q):
        part = x_from(l, q)
        return remote(part, part, sib_send.at[l, q], sib_recv.at[l, q], (s, sib))

    def owner_sends(k):
        @pl.when(s == k)
        def _():
            for i in range(LS):
                for dy in range(1, nseg):
                    w_copy(i, k * LS + i, dy).start()
                if i == 0:
                    for dy in range(1, nseg):
                        s_copy(k, dy).start()
                for dy in range(1, nseg):
                    c_copy(i, k * LS + i, dy).start()

    def relay(k):
        @pl.when(s != k)
        def _():
            for i in range(LS):
                l = k * LS + i
                w_copy(i, l, 1).wait_recv()
                for dx in range(1, xc):
                    x_copy(l, dx).start()
                sib_copy(l, 0).start()
            for i in range(LS):
                l = k * LS + i
                for dx in range(1, xc):
                    x_copy(l, dx).wait_recv()
                    sib_copy(l, dx).start()

    def wait_weights(k, i):
        @pl.when(s != k)
        def _():
            l = k * LS + i
            for q in range(xc):
                sib_copy(l, q).wait_recv()
            c_copy(i, l, 1).wait_recv()

    def ex_copy(l, pos):
        peer = (s, sib) if pos == 0 else (s, anti)
        return remote(snd.at[l], rcv.at[l], ex_send.at[l], ex_recv.at[l], peer)

    def out_copy(k):
        dy = (k + nseg - s) % nseg
        return remote(hsec.at[k + 1], out.at[0, s], o_send.at[k], o_recv.at[dy], (k, d))

    def out_local(k):
        return pltpu.make_async_copy(hsec.at[k + 1], out.at[0, s], o_loc)

    owner_sends(0)

    load_t.wait()
    for r in range(nblk):
        for c in range(nblk):
            acc = jnp.zeros((tile, tile), F32)
            for k in range(nslot):
                live = (cols[r, k] == c) & (counts[r] > k)
                acc = acc + jnp.where(live, tiles[r, k].astype(F32), F32(0.0))
            adj[r * tile : (r + 1) * tile, c * tile : (c + 1) * tile] = acc.astype(BF16)
    load_h.wait()
    load_w.wait()
    load_c.wait()

    relay(0)

    def layer(k, pos, src, dst):
        l = k * LS + pos
        gain_row = small[l, 1:2, :]
        bias_row = small[l, 0:1, :]
        for r in range(0, nodes, 64):
            hf = src[r : r + 64, :].astype(F32)
            ms = jnp.mean(hf * hf, axis=-1, keepdims=True)
            xb[r : r + 64, :] = (hf * lax.rsqrt(ms + 1e-5) * gain_row).astype(BF16)
        listed = jnp.broadcast_to(small[l, 2:3, 0:bound], (bound, bound)).T
        lane = lax.broadcasted_iota(jnp.int32, (bound, bound), 1).astype(F32)
        sent = jnp.zeros((bound, width), F32)
        for c in range(0, nodes, bound):
            pick = jnp.where(listed == lane + F32(c), F32(1.0), F32(0.0)).astype(BF16)
            sent = sent + dot(pick, xb[c : c + bound, :])
        snd[l] = sent.astype(BF16)
        ex_copy(l, pos).start()
        wait_weights(k, pos)
        for r in range(0, nodes, tile):
            t = dot(adj[r : r + tile, :], xb[...]).astype(BF16)
            z = dot(xb[r : r + tile, :], wbuf[l, 0:width, :])
            zp[r : r + tile, :] = z + dot(t, wbuf[l, width:depth, :]) + bias_row
        if pos == LS - 1:

            @pl.when(k < nseg - 1)
            def _():
                relay(k + 1)

        ex_copy(l, pos).wait_recv()
        y = dot(rcv[l], wbuf[l, width:depth, :]).astype(BF16)
        for r in range(0, nodes, tile):
            z = zp[r : r + tile, :] + dot(cbuf[l, r : r + tile, :], y)
            half = z * F32(0.5)
            gate = half + half * jnp.tanh(half)
            dst[r : r + tile, :] = (src[r : r + tile, :].astype(F32) + gate).astype(BF16)

    def section(k, carry):
        owner_sends(k + 1)

        @pl.when(s != k)
        def _():
            s_copy(k, 1).wait_recv()

        layer(k, 0, hsec.at[k], hmid)
        layer(k, 1, hmid, hsec.at[k + 1])

        @pl.when(s == k)
        def _():
            out_local(k).start()

        @pl.when(s != k)
        def _():
            out_copy(k).start()

        return carry

    lax.fori_loop(0, nseg, section, 0)

    for i in range(LS):
        for dy in range(1, nseg):
            w_copy(i, s * LS + i, dy).wait_send()
            c_copy(i, s * LS + i, dy).wait_send()
    for dy in range(1, nseg):
        s_copy(s, dy).wait_send()

    def drain(k, carry):
        for i in range(LS):
            l = k * LS + i
            ex_copy(l, i).wait_send()

            @pl.when(s != k)
            def _():
                for q in range(xc):
                    sib_copy(l, q).wait_send()
                for dx in range(1, xc):
                    x_copy(l, dx).wait_send()

        @pl.when(s != k)
        def _():
            out_copy(k).wait_send()

        return carry

    lax.fori_loop(0, nseg, drain, 0)
    out_local(s).wait()
    for dy in range(1, nseg):
        from_seg = (s + nseg - dy) % nseg
        remote(
            hsec.at[0], out.at[0, from_seg], o_send.at[0], o_recv.at[dy], yid(dy)
        ).wait_recv()


def shards(nseg, ndom, xc, feat, wts, bias, gain, tiles, cols, counts, cross, rows):
    micro, nodes, width = feat.shape
    depth = wts.shape[1]
    nblk, nslot, tile = tiles.shape[0], tiles.shape[1], tiles.shape[2]
    bound = rows.shape[1]
    layers = LS * nseg
    cross = cross.reshape(LS, nodes, bound)
    dma = pltpu.SemaphoreType.DMA
    anyspec = pl.BlockSpec(memory_space=pl.ANY)
    vspec = pl.BlockSpec(memory_space=pltpu.VMEM)
    sspec = pl.BlockSpec(memory_space=pltpu.SMEM)
    return pl.pallas_call(
        functools.partial(body, nseg, ndom, xc),
        out_shape=jax.ShapeDtypeStruct((1, micro, nodes, width), BF16),
        in_specs=[anyspec, anyspec, vspec, vspec, anyspec, sspec, sspec, anyspec, vspec],
        out_specs=anyspec,
        scratch_shapes=[
            pltpu.VMEM((layers, depth, width), BF16),
            pltpu.VMEM((layers, nodes, bound), BF16),
            pltpu.VMEM((layers, 8, width), F32),
            pltpu.VMEM((nseg + 1, nodes, width), BF16),
            pltpu.VMEM((nodes, width), BF16),
            pltpu.VMEM((nodes, width), BF16),
            pltpu.VMEM((nodes, nodes), BF16),
            pltpu.VMEM((nblk, nslot, tile, tile), BF16),
            pltpu.VMEM((layers, bound, width), BF16),
            pltpu.VMEM((layers, bound, width), BF16),
            pltpu.VMEM((nodes, width), F32),
            dma((4,)),
            dma((layers,)),
            dma((layers,)),
            dma((LS, nseg)),
            dma((layers,)),
            dma((LS, nseg)),
            dma((layers,)),
            dma((nseg,)),
            dma((nseg,)),
            dma((layers, xc)),
            dma((layers, xc)),
            dma((layers, xc)),
            dma((layers, xc)),
            dma((nseg,)),
            dma((nseg,)),
            dma,
        ],
        compiler_params=pltpu.CompilerParams(
            collective_id=0, has_side_effects=True, vmem_limit_bytes=48 << 20
        ),
        name="relay",
    )(feat, wts, bias, gain, tiles, cols, counts, cross, rows)


def solution(mesh):
    in_specs = (
        P(None, "dom", None),
        P("segment", None, None),
        P("segment", None),
        P("segment", None),
        P("dom", None, None, None),
        P("dom", None),
        P("dom"),
        P("segment", "dom", None, None),
        P("segment", "dom"),
    )
    out_specs = P("segment", None, "dom", None)
    nseg, ndom = mesh.shape["segment"], mesh.shape["dom"]
    xc = X_CHIPS if ndom >= 4 * X_CHIPS else 2
    return jax.shard_map(
        functools.partial(shards, nseg, ndom, xc),
        mesh=mesh,
        in_specs=in_specs,
        out_specs=out_specs,
        check_vma=False,
    )
```

```python
import functools

import jax
import jax.numpy as jnp
from jax import lax
from jax.experimental import pallas as pl
from jax.experimental.pallas import tpu as pltpu
from jax.sharding import PartitionSpec as P

LS = 2
X_CHIPS = 4
MESH = pl.DeviceIdType.MESH
F32 = jnp.float32
BF16 = jnp.bfloat16


def dot(a, b):
    return jnp.dot(a, b, preferred_element_type=F32)


def body(
    nseg,
    ndom,
    xc,
    feat,
    wts,
    bias_hbm,
    gain_hbm,
    tiles_hbm,
    cols,
    counts,
    cross_hbm,
    rows_hbm,
    out,
    bias,
    gain,
    rows,
    wbuf,
    cbuf,
    small,
    hsec,
    hmid,
    xb,
    adj,
    tiles,
    snd,
    rcv,
    zp,
    loc_sem,
    ex_send,
    ex_recv,
    y_send,
    y_recv,
    c_send,
    c_recv,
    s_send,
    s_recv,
    x_send,
    x_recv,
    sib_send,
    sib_recv,
    o_send,
    o_recv,
    o_loc,
):
    s = lax.axis_index("segment")
    d = lax.axis_index("dom")
    core = d % 2
    xi = (d // 2) % xc
    base = d - (d % (2 * xc))
    sib = base + xi * 2 + (1 - core)
    anti = (d + ndom // 2) % ndom
    depth, width = wbuf.shape[1], wbuf.shape[2]
    nblk, nslot, tile = tiles_hbm.shape[0], tiles_hbm.shape[1], tiles_hbm.shape[2]
    nodes = nblk * tile
    bound = rows.shape[1]
    shard = depth // (2 * xc)
    mine = (xi * 2 + core) * shard

    def yid(dy):
        return ((s + dy) % nseg, d)

    def xid(dx):
        return (s, base + ((xi + dx) % xc) * 2 + core)

    load_h = pltpu.make_async_copy(feat.at[s], hsec.at[0], loc_sem.at[0])
    load_w = pltpu.make_async_copy(wts, wbuf.at[pl.ds(s * LS, LS)], loc_sem.at[1])
    load_c = pltpu.make_async_copy(cross_hbm, cbuf.at[pl.ds(s * LS, LS)], loc_sem.at[2])
    load_t = pltpu.make_async_copy(tiles_hbm, tiles, loc_sem.at[3])
    loads = [
        pltpu.make_async_copy(a, b, loc_sem.at[4 + i])
        for i, (a, b) in enumerate(((bias_hbm, bias), (gain_hbm, gain), (rows_hbm, rows)))
    ]
    for load in loads:
        load.start()
    load_t.start()
    load_h.start()
    load_w.start()
    load_c.start()

    for load in loads:
        load.wait()
    for i in range(LS):
        small[s * LS + i] = jnp.zeros((8, width), F32)
        small[s * LS + i, 0:1, :] = bias[i : i + 1, :]
        small[s * LS + i, 1:2, :] = gain[i : i + 1, :]
        small[s * LS + i, 2:3, 0:bound] = rows[i : i + 1, :].astype(F32)

    barrier = pltpu.get_barrier_semaphore()
    peers = [yid(dy) for dy in range(1, nseg)]
    peers += [xid(dx) for dx in range(1, xc)]
    peers += [(s, sib), (s, anti)]
    for peer in peers:
        pl.semaphore_signal(barrier, inc=1, device_id=peer, device_id_type=MESH)
    pl.semaphore_wait(barrier, len(peers))

    def remote(src, dst, send, recv, peer):
        return pltpu.make_async_remote_copy(
            src_ref=src,
            dst_ref=dst,
            send_sem=send,
            recv_sem=recv,
            device_id=peer,
            device_id_type=MESH,
        )

    def w_copy(i, l, dy):
        return remote(
            wts.at[i, pl.ds(mine, shard)],
            wbuf.at[l, pl.ds(mine, shard)],
            y_send.at[i, dy],
            y_recv.at[l],
            yid(dy),
        )

    def c_copy(i, l, dy):
        return remote(cross_hbm.at[i], cbuf.at[l], c_send.at[i, dy], c_recv.at[l], yid(dy))

    def s_copy(k, dy):
        part = small.at[pl.ds(k * LS, LS)]
        return remote(part, part, s_send.at[dy], s_recv.at[k], yid(dy))

    def x_copy(l, dx):
        part = wbuf.at[l, pl.ds(mine, shard)]
        return remote(part, part, x_send.at[l, dx], x_recv.at[l, dx], xid(dx))

    def x_from(l, dx):
        start = (((xi + xc - dx) % xc) * 2 + core) * shard
        return wbuf.at[l, pl.ds(start, shard)]

    def sib_copy(l, q):
        part = x_from(l, q)
        return remote(part, part, sib_send.at[l, q], sib_recv.at[l, q], (s, sib))

    def owner_sends(k):
        @pl.when(s == k)
        def _():
            for i in range(LS):
                for dy in range(1, nseg):
                    w_copy(i, k * LS + i, dy).start()
                if i == 0:
                    for dy in range(1, nseg):
                        s_copy(k, dy).start()
                for dy in range(1, nseg):
                    c_copy(i, k * LS + i, dy).start()

    def spread(k, i):
        @pl.when((s != k) & (k < nseg))
        def _():
            l = k * LS + i
            w_copy(i, l, 1).wait_recv()
            for dx in range(1, xc):
                x_copy(l, dx).start()
            sib_copy(l, 0).start()

    def share(k, i):
        @pl.when((s != k) & (k < nseg))
        def _():
            l = k * LS + i
            for dx in range(1, xc):
                x_copy(l, dx).wait_recv()
                sib_copy(l, dx).start()

    def wait_weights(k, i):
        @pl.when(s != k)
        def _():
            l = k * LS + i
            for q in range(xc):
                sib_copy(l, q).wait_recv()
            c_copy(i, l, 1).wait_recv()

    def ex_copy(l, pos):
        peer = (s, sib) if pos == 0 else (s, anti)
        return remote(snd.at[l], rcv.at[l], ex_send.at[l], ex_recv.at[l], peer)

    def out_copy(k, b):
        dy = (k + nseg - s) % nseg
        part = pl.ds(b * tile, tile)
        return remote(
            hsec.at[k + 1, part],
            out.at[0, s, part],
            o_send.at[k, b],
            o_recv.at[dy, b],
            (k, d),
        )

    def out_local(k, b):
        part = pl.ds(b * tile, tile)
        return pltpu.make_async_copy(hsec.at[k + 1, part], out.at[0, s, part], o_loc.at[b])

    owner_sends(0)

    load_t.wait()
    for r in range(nblk):
        for c in range(nblk):
            acc = jnp.zeros((tile, tile), F32)
            for k in range(nslot):
                live = (cols[r, k] == c) & (counts[r] > k)
                acc = acc + jnp.where(live, tiles[r, k].astype(F32), F32(0.0))
            adj[r * tile : (r + 1) * tile, c * tile : (c + 1) * tile] = acc.astype(BF16)
    load_h.wait()
    load_w.wait()
    load_c.wait()

    spread(0, 0)
    owner_sends(1)
    spread(0, 1)
    share(0, 0)

    def send_out(k, b):
        @pl.when(s == k)
        def _():
            out_local(k, b).start()

        @pl.when(s != k)
        def _():
            out_copy(k, b).start()

    def layer(k, pos, src, dst):
        l = k * LS + pos
        gain_row = small[l, 1:2, :]
        bias_row = small[l, 0:1, :]
        for r in range(0, nodes, 64):
            hf = src[r : r + 64, :].astype(F32)
            ms = jnp.mean(hf * hf, axis=-1, keepdims=True)
            xb[r : r + 64, :] = (hf * lax.rsqrt(ms + 1e-5) * gain_row).astype(BF16)
        listed = jnp.broadcast_to(small[l, 2:3, 0:bound], (bound, bound)).T
        lane = lax.broadcasted_iota(jnp.int32, (bound, bound), 1).astype(F32)
        sent = jnp.zeros((bound, width), F32)
        for c in range(0, nodes, bound):
            pick = jnp.where(listed == lane + F32(c), F32(1.0), F32(0.0)).astype(BF16)
            sent = sent + dot(pick, xb[c : c + bound, :])
        snd[l] = sent.astype(BF16)
        ex_copy(l, pos).start()
        wait_weights(k, pos)
        for r in range(0, nodes, tile):
            t = dot(adj[r : r + tile, :], xb[...]).astype(BF16)
            z = dot(xb[r : r + tile, :], wbuf[l, 0:width, :])
            zp[r : r + tile, :] = z + dot(t, wbuf[l, width:depth, :]) + bias_row
        spread(k + 1, pos)
        if pos < LS - 1:
            share(k, pos + 1)
        else:
            share(k + 1, 0)
        ex_copy(l, pos).wait_recv()
        y = dot(rcv[l], wbuf[l, width:depth, :]).astype(BF16)
        for r in range(0, nodes, tile):
            z = zp[r : r + tile, :] + dot(cbuf[l, r : r + tile, :], y)
            half = z * F32(0.5)
            gate = half + half * jnp.tanh(half)
            dst[r : r + tile, :] = (src[r : r + tile, :].astype(F32) + gate).astype(BF16)
            if pos == LS - 1:
                send_out(k, r // tile)

    def section(k, carry):
        owner_sends(k + 2)

        @pl.when(s != k)
        def _():
            s_copy(k, 1).wait_recv()

        layer(k, 0, hsec.at[k], hmid)
        layer(k, 1, hmid, hsec.at[k + 1])
        return carry

    lax.fori_loop(0, nseg, section, 0)

    for i in range(LS):
        for dy in range(1, nseg):
            w_copy(i, s * LS + i, dy).wait_send()
            c_copy(i, s * LS + i, dy).wait_send()
    for dy in range(1, nseg):
        s_copy(s, dy).wait_send()

    def drain(k, carry):
        for i in range(LS):
            l = k * LS + i
            ex_copy(l, i).wait_send()

            @pl.when(s != k)
            def _():
                for q in range(xc):
                    sib_copy(l, q).wait_send()
                for dx in range(1, xc):
                    x_copy(l, dx).wait_send()

        @pl.when(s != k)
        def _():
            for b in range(nblk):
                out_copy(k, b).wait_send()

        return carry

    lax.fori_loop(0, nseg, drain, 0)
    for b in range(nblk):
        out_local(s, b).wait()
    for dy in range(1, nseg):
        from_seg = (s + nseg - dy) % nseg
        for b in range(nblk):
            part = pl.ds(b * tile, tile)
            remote(
                hsec.at[0, part],
                out.at[0, from_seg, part],
                o_send.at[0, b],
                o_recv.at[dy, b],
                yid(dy),
            ).wait_recv()


def shards(nseg, ndom, xc, feat, wts, bias, gain, tiles, cols, counts, cross, rows):
    micro, nodes, width = feat.shape
    depth = wts.shape[1]
    nblk, nslot, tile = tiles.shape[0], tiles.shape[1], tiles.shape[2]
    bound = rows.shape[1]
    layers = LS * nseg
    cross = cross.reshape(LS, nodes, bound)
    dma = pltpu.SemaphoreType.DMA
    anyspec = pl.BlockSpec(memory_space=pltpu.HBM)
    sspec = pl.BlockSpec(memory_space=pltpu.SMEM)
    return pl.pallas_call(
        functools.partial(body, nseg, ndom, xc),
        out_shape=jax.ShapeDtypeStruct((1, micro, nodes, width), BF16),
        in_specs=[anyspec, anyspec, anyspec, anyspec, anyspec, sspec, sspec, anyspec, anyspec],
        out_specs=pl.BlockSpec(memory_space=pl.ANY),
        scratch_shapes=[
            pltpu.VMEM((LS, width), F32),
            pltpu.VMEM((LS, width), F32),
            pltpu.VMEM((LS, bound), jnp.int32),
            pltpu.VMEM((layers, depth, width), BF16),
            pltpu.VMEM((layers, nodes, bound), BF16),
            pltpu.VMEM((layers, 8, width), F32),
            pltpu.VMEM((nseg + 1, nodes, width), BF16),
            pltpu.VMEM((nodes, width), BF16),
            pltpu.VMEM((nodes, width), BF16),
            pltpu.VMEM((nodes, nodes), BF16),
            pltpu.VMEM((nblk, nslot, tile, tile), BF16),
            pltpu.VMEM((layers, bound, width), BF16),
            pltpu.VMEM((layers, bound, width), BF16),
            pltpu.VMEM((nodes, width), F32),
            dma((7,)),
            dma((layers,)),
            dma((layers,)),
            dma((LS, nseg)),
            dma((layers,)),
            dma((LS, nseg)),
            dma((layers,)),
            dma((nseg,)),
            dma((nseg,)),
            dma((layers, xc)),
            dma((layers, xc)),
            dma((layers, xc)),
            dma((layers, xc)),
            dma((nseg, nblk)),
            dma((nseg, nblk)),
            dma((nblk,)),
        ],
        compiler_params=pltpu.CompilerParams(
            collective_id=0, has_side_effects=True, vmem_limit_bytes=48 << 20
        ),
        name="relay",
    )(feat, wts, bias, gain, tiles, cols, counts, cross, rows)


def solution(mesh):
    in_specs = (
        P(None, "dom", None),
        P("segment", None, None),
        P("segment", None),
        P("segment", None),
        P("dom", None, None, None),
        P("dom", None),
        P("dom"),
        P("segment", "dom", None, None),
        P("segment", "dom"),
    )
    out_specs = P("segment", None, "dom", None)
    nseg, ndom = mesh.shape["segment"], mesh.shape["dom"]
    xc = X_CHIPS if ndom >= 4 * X_CHIPS else 2
    return jax.shard_map(
        functools.partial(shards, nseg, ndom, xc),
        mesh=mesh,
        in_specs=in_specs,
        out_specs=out_specs,
        check_vma=False,
    )
```

```python
import functools

import jax
import jax.numpy as jnp
from jax import lax
from jax.experimental import pallas as pl
from jax.experimental.pallas import tpu as pltpu
from jax.sharding import PartitionSpec as P

LS = 2
X_CHIPS = 4
MESH = pl.DeviceIdType.MESH
F32 = jnp.float32
BF16 = jnp.bfloat16


def dot(a, b):
    return jnp.dot(a, b, preferred_element_type=F32)


def body(
    nseg,
    ndom,
    xc,
    feat,
    wts,
    bias_hbm,
    gain_hbm,
    tiles_hbm,
    cols_hbm,
    counts_hbm,
    cross_hbm,
    rows_hbm,
    out,
    cols,
    counts,
    bias,
    gain,
    rows,
    wbuf,
    cbuf,
    small,
    hsec,
    hmid,
    xb,
    adj,
    tiles,
    snd,
    rcv,
    zp,
    loc_sem,
    ex_send,
    ex_recv,
    y_send,
    y_recv,
    c_send,
    c_recv,
    s_send,
    s_recv,
    x_send,
    x_recv,
    sib_send,
    sib_recv,
    o_send,
    o_recv,
    o_loc,
):
    s = lax.axis_index("segment")
    d = lax.axis_index("dom")
    core = d % 2
    xi = (d // 2) % xc
    base = d - (d % (2 * xc))
    sib = base + xi * 2 + (1 - core)
    anti = (d + ndom // 2) % ndom
    depth, width = wbuf.shape[1], wbuf.shape[2]
    nblk, nslot, tile = tiles_hbm.shape[0], tiles_hbm.shape[1], tiles_hbm.shape[2]
    nodes = nblk * tile
    bound = rows.shape[1]
    shard = depth // (2 * xc)
    mine = (xi * 2 + core) * shard

    def yid(dy):
        return ((s + dy) % nseg, d)

    def xid(dx):
        return (s, base + ((xi + dx) % xc) * 2 + core)

    load_h = pltpu.make_async_copy(feat.at[s], hsec.at[0], loc_sem.at[0])
    load_w = pltpu.make_async_copy(wts, wbuf.at[pl.ds(s * LS, LS)], loc_sem.at[1])
    load_c = pltpu.make_async_copy(cross_hbm, cbuf.at[pl.ds(s * LS, LS)], loc_sem.at[2])
    load_t = pltpu.make_async_copy(tiles_hbm, tiles, loc_sem.at[3])
    loads = [
        pltpu.make_async_copy(a, b, loc_sem.at[4 + i])
        for i, (a, b) in enumerate(
            (
                (bias_hbm, bias),
                (gain_hbm, gain),
                (rows_hbm, rows),
                (cols_hbm, cols),
                (counts_hbm, counts),
            )
        )
    ]
    for load in loads:
        load.start()
    load_t.start()
    load_h.start()
    load_w.start()
    load_c.start()

    for load in loads:
        load.wait()
    for i in range(LS):
        small[s * LS + i] = jnp.zeros((8, width), F32)
        small[s * LS + i, 0:1, :] = bias[i : i + 1, :]
        small[s * LS + i, 1:2, :] = gain[i : i + 1, :]
        small[s * LS + i, 2:3, 0:bound] = rows[i : i + 1, :].astype(F32)

    barrier = pltpu.get_barrier_semaphore()
    peers = [yid(dy) for dy in range(1, nseg)]
    peers += [xid(dx) for dx in range(1, xc)]
    peers += [(s, sib), (s, anti)]
    for peer in peers:
        pl.semaphore_signal(barrier, inc=1, device_id=peer, device_id_type=MESH)
    pl.semaphore_wait(barrier, len(peers))

    def remote(src, dst, send, recv, peer):
        return pltpu.make_async_remote_copy(
            src_ref=src,
            dst_ref=dst,
            send_sem=send,
            recv_sem=recv,
            device_id=peer,
            device_id_type=MESH,
        )

    def w_copy(i, l, dy):
        return remote(
            wts.at[i, pl.ds(mine, shard)],
            wbuf.at[l, pl.ds(mine, shard)],
            y_send.at[i, dy],
            y_recv.at[l],
            yid(dy),
        )

    def c_copy(i, l, dy):
        return remote(cross_hbm.at[i], cbuf.at[l], c_send.at[i, dy], c_recv.at[l], yid(dy))

    def s_copy(k, dy):
        part = small.at[pl.ds(k * LS, LS)]
        return remote(part, part, s_send.at[dy], s_recv.at[k], yid(dy))

    def x_copy(l, dx):
        part = wbuf.at[l, pl.ds(mine, shard)]
        return remote(part, part, x_send.at[l, dx], x_recv.at[l, dx], xid(dx))

    def x_from(l, dx):
        start = (((xi + xc - dx) % xc) * 2 + core) * shard
        return wbuf.at[l, pl.ds(start, shard)]

    def sib_copy(l, q):
        part = x_from(l, q)
        return remote(part, part, sib_send.at[l, q], sib_recv.at[l, q], (s, sib))

    order = sorted(range(1, nseg), key=lambda dy: min(dy, nseg - dy))

    def owner_sends(k):
        @pl.when(s == k)
        def _():
            for i in range(LS):
                for dy in order:
                    w_copy(i, k * LS + i, dy).start()
                if i == 0:
                    for dy in order:
                        s_copy(k, dy).start()
            for i in range(LS):
                for dy in order:
                    c_copy(i, k * LS + i, dy).start()

    def spread(k, i):
        @pl.when((s != k) & (k < nseg))
        def _():
            l = k * LS + i
            w_copy(i, l, 1).wait_recv()
            for dx in range(1, xc):
                x_copy(l, dx).start()
            sib_copy(l, 0).start()

    def share(k, i):
        @pl.when((s != k) & (k < nseg))
        def _():
            l = k * LS + i
            for dx in range(1, xc):
                x_copy(l, dx).wait_recv()
                sib_copy(l, dx).start()

    def wait_weights(k, i):
        @pl.when(s != k)
        def _():
            l = k * LS + i
            for q in range(xc):
                sib_copy(l, q).wait_recv()
            c_copy(i, l, 1).wait_recv()

    def ex_copy(l, pos):
        peer = (s, sib) if pos == 0 else (s, anti)
        return remote(snd.at[l], rcv.at[l], ex_send.at[l], ex_recv.at[l], peer)

    def out_copy(k, b):
        dy = (k + nseg - s) % nseg
        part = pl.ds(b * tile, tile)
        return remote(
            hsec.at[k + 1, part],
            out.at[0, s, part],
            o_send.at[k, b],
            o_recv.at[dy, b],
            (k, d),
        )

    def out_local(k, b):
        part = pl.ds(b * tile, tile)
        return pltpu.make_async_copy(hsec.at[k + 1, part], out.at[0, s, part], o_loc.at[b])

    owner_sends(0)

    load_t.wait()
    for r in range(nblk):
        for c in range(nblk):
            acc = jnp.zeros((tile, tile), F32)
            for k in range(nslot):
                live = (cols[r, k] == c) & (counts[r] > k)
                acc = acc + jnp.where(live, tiles[r, k].astype(F32), F32(0.0))
            adj[r * tile : (r + 1) * tile, c * tile : (c + 1) * tile] = acc.astype(BF16)
    load_h.wait()
    load_w.wait()
    load_c.wait()

    spread(0, 0)
    owner_sends(1)
    spread(0, 1)
    share(0, 0)

    def send_out(k, b):
        @pl.when(s == k)
        def _():
            out_local(k, b).start()

        @pl.when(s != k)
        def _():
            out_copy(k, b).start()

    def layer(k, pos, src, dst):
        l = k * LS + pos
        gain_row = small[l, 1:2, :]
        bias_row = small[l, 0:1, :]
        for r in range(0, nodes, 64):
            hf = src[r : r + 64, :].astype(F32)
            ms = jnp.mean(hf * hf, axis=-1, keepdims=True)
            xb[r : r + 64, :] = (hf * lax.rsqrt(ms + 1e-5) * gain_row).astype(BF16)
        listed = jnp.broadcast_to(small[l, 2:3, 0:bound], (bound, bound)).T
        lane = lax.broadcasted_iota(jnp.int32, (bound, bound), 1).astype(F32)
        sent = jnp.zeros((bound, width), F32)
        for c in range(0, nodes, bound):
            pick = jnp.where(listed == lane + F32(c), F32(1.0), F32(0.0)).astype(BF16)
            sent = sent + dot(pick, xb[c : c + bound, :])
        snd[l] = sent.astype(BF16)
        ex_copy(l, pos).start()
        wait_weights(k, pos)
        for r in range(0, nodes, tile):
            t = dot(adj[r : r + tile, :], xb[...]).astype(BF16)
            z = dot(xb[r : r + tile, :], wbuf[l, 0:width, :])
            zp[r : r + tile, :] = z + dot(t, wbuf[l, width:depth, :]) + bias_row
        spread(k + 1, pos)
        if pos < LS - 1:
            share(k, pos + 1)
        else:
            share(k + 1, 0)
        ex_copy(l, pos).wait_recv()
        y = dot(rcv[l], wbuf[l, width:depth, :]).astype(BF16)
        for r in range(0, nodes, tile):
            z = zp[r : r + tile, :] + dot(cbuf[l, r : r + tile, :], y)
            half = z * F32(0.5)
            gate = half + half * jnp.tanh(half)
            dst[r : r + tile, :] = (src[r : r + tile, :].astype(F32) + gate).astype(BF16)
            if pos == LS - 1:
                send_out(k, r // tile)

    def section(k, carry):
        owner_sends(k + 2)

        @pl.when(s != k)
        def _():
            s_copy(k, 1).wait_recv()

        layer(k, 0, hsec.at[k], hmid)
        layer(k, 1, hmid, hsec.at[k + 1])
        return carry

    lax.fori_loop(0, nseg, section, 0)

    for i in range(LS):
        for dy in range(1, nseg):
            w_copy(i, s * LS + i, dy).wait_send()
            c_copy(i, s * LS + i, dy).wait_send()
    for dy in range(1, nseg):
        s_copy(s, dy).wait_send()

    def drain(k, carry):
        for i in range(LS):
            l = k * LS + i
            ex_copy(l, i).wait_send()

            @pl.when(s != k)
            def _():
                for q in range(xc):
                    sib_copy(l, q).wait_send()
                for dx in range(1, xc):
                    x_copy(l, dx).wait_send()

        @pl.when(s != k)
        def _():
            for b in range(nblk):
                out_copy(k, b).wait_send()

        return carry

    lax.fori_loop(0, nseg, drain, 0)
    for b in range(nblk):
        out_local(s, b).wait()
    for dy in range(1, nseg):
        from_seg = (s + nseg - dy) % nseg
        for b in range(nblk):
            part = pl.ds(b * tile, tile)
            remote(
                hsec.at[0, part],
                out.at[0, from_seg, part],
                o_send.at[0, b],
                o_recv.at[dy, b],
                yid(dy),
            ).wait_recv()


def hbm(a):
    return pltpu.with_memory_space_constraint(a, pltpu.HBM)


def shards(nseg, ndom, xc, feat, wts, bias, gain, tiles, cols, counts, cross, rows):
    micro, nodes, width = feat.shape
    depth = wts.shape[1]
    nblk, nslot, tile = tiles.shape[0], tiles.shape[1], tiles.shape[2]
    bound = rows.shape[1]
    layers = LS * nseg
    cross = cross.reshape(LS, nodes, bound)
    dma = pltpu.SemaphoreType.DMA
    anyspec = pl.BlockSpec(memory_space=pltpu.HBM)
    return pl.pallas_call(
        functools.partial(body, nseg, ndom, xc),
        out_shape=jax.ShapeDtypeStruct((1, micro, nodes, width), BF16),
        in_specs=[anyspec] * 9,
        out_specs=pl.BlockSpec(memory_space=pl.ANY),
        scratch_shapes=[
            pltpu.SMEM(cols.shape, jnp.int32),
            pltpu.SMEM(counts.shape, jnp.int32),
            pltpu.VMEM((LS, width), F32),
            pltpu.VMEM((LS, width), F32),
            pltpu.VMEM((LS, bound), jnp.int32),
            pltpu.VMEM((layers, depth, width), BF16),
            pltpu.VMEM((layers, nodes, bound), BF16),
            pltpu.VMEM((layers, 8, width), F32),
            pltpu.VMEM((nseg + 1, nodes, width), BF16),
            pltpu.VMEM((nodes, width), BF16),
            pltpu.VMEM((nodes, width), BF16),
            pltpu.VMEM((nodes, nodes), BF16),
            pltpu.VMEM((nblk, nslot, tile, tile), BF16),
            pltpu.VMEM((layers, bound, width), BF16),
            pltpu.VMEM((layers, bound, width), BF16),
            pltpu.VMEM((nodes, width), F32),
            dma((9,)),
            dma((layers,)),
            dma((layers,)),
            dma((LS, nseg)),
            dma((layers,)),
            dma((LS, nseg)),
            dma((layers,)),
            dma((nseg,)),
            dma((nseg,)),
            dma((layers, xc)),
            dma((layers, xc)),
            dma((layers, xc)),
            dma((layers, xc)),
            dma((nseg, nblk)),
            dma((nseg, nblk)),
            dma((nblk,)),
        ],
        compiler_params=pltpu.CompilerParams(
            collective_id=0, has_side_effects=True, vmem_limit_bytes=48 << 20
        ),
        name="relay",
    )(*(hbm(a) for a in (feat, wts, bias, gain, tiles, cols, counts, cross, rows)))


def solution(mesh):
    in_specs = (
        P(None, "dom", None),
        P("segment", None, None),
        P("segment", None),
        P("segment", None),
        P("dom", None, None, None),
        P("dom", None),
        P("dom"),
        P("segment", "dom", None, None),
        P("segment", "dom"),
    )
    out_specs = P("segment", None, "dom", None)
    nseg, ndom = mesh.shape["segment"], mesh.shape["dom"]
    xc = X_CHIPS if ndom >= 4 * X_CHIPS else 2
    return jax.shard_map(
        functools.partial(shards, nseg, ndom, xc),
        mesh=mesh,
        in_specs=in_specs,
        out_specs=out_specs,
        check_vma=False,
    )
```

```python
import functools

import jax
import jax.numpy as jnp
from jax import lax
from jax.experimental import pallas as pl
from jax.experimental.pallas import tpu as pltpu
from jax.sharding import PartitionSpec as P

LS = 2
X_CHIPS = 4
MESH = pl.DeviceIdType.MESH
F32 = jnp.float32
BF16 = jnp.bfloat16


def dot(a, b):
    return jnp.dot(a, b, preferred_element_type=F32)


def body(
    nseg,
    ndom,
    xc,
    feat,
    wts,
    bias_hbm,
    gain_hbm,
    tiles_hbm,
    cols_hbm,
    counts_hbm,
    cross_hbm,
    rows_hbm,
    out,
    cols,
    counts,
    bias,
    gain,
    rows,
    wbuf,
    cbuf,
    small,
    hsec,
    hmid,
    xb,
    adj,
    tiles,
    snd,
    rcv,
    zp,
    loc_sem,
    ex_send,
    ex_recv,
    y_send,
    y_recv,
    c_send,
    c_recv,
    s_send,
    s_recv,
    x_send,
    x_recv,
    sib_send,
    sib_recv,
    o_send,
    o_recv,
    o_loc,
    f_send,
    f_recv,
):
    s = lax.axis_index("segment")
    d = lax.axis_index("dom")
    core = d % 2
    xi = (d // 2) % xc
    base = d - (d % (2 * xc))
    sib = base + xi * 2 + (1 - core)
    anti = (d + ndom // 2) % ndom
    depth, width = wbuf.shape[1], wbuf.shape[2]
    nblk, nslot, tile = tiles_hbm.shape[0], tiles_hbm.shape[1], tiles_hbm.shape[2]
    nodes = nblk * tile
    bound = rows.shape[1]
    shard = depth // (2 * xc)
    mine = (xi * 2 + core) * shard

    def yid(dy):
        return ((s + dy) % nseg, d)

    def xid(dx):
        return (s, base + ((xi + dx) % xc) * 2 + core)

    load_h = pltpu.make_async_copy(feat.at[s], hsec.at[0], loc_sem.at[0])
    load_w = pltpu.make_async_copy(wts, wbuf.at[pl.ds(s * LS, LS)], loc_sem.at[1])
    load_c = pltpu.make_async_copy(cross_hbm, cbuf.at[pl.ds(s * LS, LS)], loc_sem.at[2])
    load_t = pltpu.make_async_copy(tiles_hbm, tiles, loc_sem.at[3])
    loads = [
        pltpu.make_async_copy(a, b, loc_sem.at[4 + i])
        for i, (a, b) in enumerate(
            (
                (bias_hbm, bias),
                (gain_hbm, gain),
                (rows_hbm, rows),
                (cols_hbm, cols),
                (counts_hbm, counts),
            )
        )
    ]
    for load in loads:
        load.start()
    load_t.start()
    load_h.start()
    load_w.start()
    load_c.start()

    for load in loads:
        load.wait()
    for i in range(LS):
        small[s * LS + i] = jnp.zeros((8, width), F32)
        small[s * LS + i, 0:1, :] = bias[i : i + 1, :]
        small[s * LS + i, 1:2, :] = gain[i : i + 1, :]
        small[s * LS + i, 2:3, 0:bound] = rows[i : i + 1, :].astype(F32)

    barrier = pltpu.get_barrier_semaphore()
    peers = [yid(dy) for dy in range(1, nseg)]
    peers += [xid(dx) for dx in range(1, xc)]
    peers += [(s, sib), (s, anti)]
    for peer in peers:
        pl.semaphore_signal(barrier, inc=1, device_id=peer, device_id_type=MESH)
    pl.semaphore_wait(barrier, len(peers))

    def remote(src, dst, send, recv, peer):
        return pltpu.make_async_remote_copy(
            src_ref=src,
            dst_ref=dst,
            send_sem=send,
            recv_sem=recv,
            device_id=peer,
            device_id_type=MESH,
        )

    def w_copy(i, l, dy):
        return remote(
            wts.at[i, pl.ds(mine, shard)],
            wbuf.at[l, pl.ds(mine, shard)],
            y_send.at[i, dy],
            y_recv.at[l],
            yid(dy),
        )

    def c_copy(i, l, dy):
        return remote(cross_hbm.at[i], cbuf.at[l], c_send.at[i, dy], c_recv.at[l], yid(dy))

    def s_copy(k, dy):
        part = small.at[pl.ds(k * LS, LS)]
        return remote(part, part, s_send.at[dy], s_recv.at[k], yid(dy))

    def x_copy(l, dx):
        part = wbuf.at[l, pl.ds(mine, shard)]
        return remote(part, part, x_send.at[l, dx], x_recv.at[l, dx], xid(dx))

    def x_from(l, dx):
        start = (((xi + xc - dx) % xc) * 2 + core) * shard
        return wbuf.at[l, pl.ds(start, shard)]

    def sib_copy(l, q):
        part = x_from(l, q)
        return remote(part, part, sib_send.at[l, q], sib_recv.at[l, q], (s, sib))

    order = sorted(range(1, nseg), key=lambda dy: min(dy, nseg - dy))

    def owner_sends(k):
        if isinstance(k, int) and k >= nseg:
            return

        @pl.when(s == k)
        def _():
            for i in range(LS):
                for dy in order:
                    w_copy(i, k * LS + i, dy).start()
                if i == 0:
                    for dy in order:
                        s_copy(k, dy).start()
            for i in range(LS):
                for dy in order:
                    c_copy(i, k * LS + i, dy).start()

    def spread(k, i):
        if isinstance(k, int) and k >= nseg:
            return

        @pl.when((s != k) & (k < nseg))
        def _():
            l = k * LS + i
            w_copy(i, l, 1).wait_recv()
            for dx in range(1, xc):
                x_copy(l, dx).start()
            sib_copy(l, 0).start()

    def share(k, i):
        if isinstance(k, int) and k >= nseg:
            return

        @pl.when((s != k) & (k < nseg))
        def _():
            l = k * LS + i
            for dx in range(1, xc):
                x_copy(l, dx).wait_recv()
                sib_copy(l, dx).start()

    def wait_weights(k, i):
        @pl.when(s != k)
        def _():
            l = k * LS + i
            for q in range(xc):
                sib_copy(l, q).wait_recv()
            c_copy(i, l, 1).wait_recv()

    def ex_copy(l, pos):
        peer = (s, sib) if pos == 0 else (s, anti)
        return remote(snd.at[l], rcv.at[l], ex_send.at[l], ex_recv.at[l], peer)

    last = nseg - 1
    far = (last + nseg // 2) % nseg

    def far_copy(b):
        part = pl.ds(b * tile, tile)
        return remote(
            hsec.at[last, part],
            hsec.at[nseg + 1, part],
            f_send.at[b],
            f_recv.at[b],
            (last, d),
        )

    def out_copy(k, b):
        dy = (k + nseg - s) % nseg
        part = pl.ds(b * tile, tile)
        return remote(
            hsec.at[k + 1, part],
            out.at[0, s, part],
            o_send.at[k, b],
            o_recv.at[dy, b],
            (k, d),
        )

    def out_local(k, b):
        part = pl.ds(b * tile, tile)
        return pltpu.make_async_copy(hsec.at[k + 1, part], out.at[0, s, part], o_loc.at[b])

    def out_extra(b):
        part = pl.ds(b * tile, tile)
        return pltpu.make_async_copy(
            hsec.at[nseg + 2, part], out.at[0, far, part], o_loc.at[nblk + b]
        )

    owner_sends(0)

    load_t.wait()
    for r in range(nblk):
        for c in range(nblk):
            acc = jnp.zeros((tile, tile), F32)
            for k in range(nslot):
                live = (cols[r, k] == c) & (counts[r] > k)
                acc = acc + jnp.where(live, tiles[r, k].astype(F32), F32(0.0))
            adj[r * tile : (r + 1) * tile, c * tile : (c + 1) * tile] = acc.astype(BF16)
    load_h.wait()
    load_w.wait()
    load_c.wait()

    spread(0, 0)
    owner_sends(1)
    spread(0, 1)
    share(0, 0)

    def send_out(k, b):
        @pl.when(s == k)
        def _():
            out_local(k, b).start()

        @pl.when(s != k)
        def _():
            out_copy(k, b).start()

        @pl.when((s == far) & (k == last - 1))
        def _():
            far_copy(b).start()

    def layer(k, pos, src, dst, extra=False):
        l = k * LS + pos
        slot = LS * nseg + pos if extra else l
        gain_row = small[l, 1:2, :]
        bias_row = small[l, 0:1, :]
        for r in range(0, nodes, 64):
            hf = src[r : r + 64, :].astype(F32)
            ms = jnp.mean(hf * hf, axis=-1, keepdims=True)
            xb[r : r + 64, :] = (hf * lax.rsqrt(ms + 1e-5) * gain_row).astype(BF16)
        listed = jnp.broadcast_to(small[l, 2:3, 0:bound], (bound, bound)).T
        lane = lax.broadcasted_iota(jnp.int32, (bound, bound), 1).astype(F32)
        sent = jnp.zeros((bound, width), F32)
        for c in range(0, nodes, bound):
            pick = jnp.where(listed == lane + F32(c), F32(1.0), F32(0.0)).astype(BF16)
            sent = sent + dot(pick, xb[c : c + bound, :])
        snd[slot] = sent.astype(BF16)
        ex_copy(slot, pos).start()
        if not extra:
            wait_weights(k, pos)
        for r in range(0, nodes, tile):
            t = dot(adj[r : r + tile, :], xb[...]).astype(BF16)
            z = dot(xb[r : r + tile, :], wbuf[l, 0:width, :])
            zp[r : r + tile, :] = z + dot(t, wbuf[l, width:depth, :]) + bias_row
        if not extra:
            spread(k + 1, pos)
            if pos < LS - 1:
                share(k, pos + 1)
            else:
                share(k + 1, 0)
        ex_copy(slot, pos).wait_recv()
        y = dot(rcv[slot], wbuf[l, width:depth, :]).astype(BF16)
        for r in range(0, nodes, tile):
            z = zp[r : r + tile, :] + dot(cbuf[l, r : r + tile, :], y)
            half = z * F32(0.5)
            gate = half + half * jnp.tanh(half)
            dst[r : r + tile, :] = (src[r : r + tile, :].astype(F32) + gate).astype(BF16)
            if extra and pos == LS - 1:
                out_extra(r // tile).start()
            elif pos == LS - 1:
                send_out(k, r // tile)

    def section(k, carry):
        owner_sends(k + 2)

        @pl.when(s != k)
        def _():
            s_copy(k, 1).wait_recv()

        layer(k, 0, hsec.at[k], hmid)
        layer(k, 1, hmid, hsec.at[k + 1])
        return carry

    lax.fori_loop(0, last, section, 0)

    @pl.when(s == far)
    def _():
        s_copy(last, 1).wait_recv()
        wait_weights(last, 0)
        share(last, 1)
        wait_weights(last, 1)

    @pl.when(s != far)
    def _():
        section(last, 0)

    @pl.when(s == last)
    def _():
        for b in range(nblk):
            far_copy(b).wait_recv()
        layer(last, 0, hsec.at[nseg + 1], hmid, extra=True)
        layer(last, 1, hmid, hsec.at[nseg + 2], extra=True)

    for i in range(LS):
        for dy in range(1, nseg):
            w_copy(i, s * LS + i, dy).wait_send()
            c_copy(i, s * LS + i, dy).wait_send()
    for dy in range(1, nseg):
        s_copy(s, dy).wait_send()

    def drain(k, carry):
        for i in range(LS):
            l = k * LS + i

            @pl.when((s != far) | (k != last))
            def _():
                ex_copy(l, i).wait_send()

            @pl.when(s != k)
            def _():
                for q in range(xc):
                    sib_copy(l, q).wait_send()
                for dx in range(1, xc):
                    x_copy(l, dx).wait_send()

        @pl.when((s != k) & ((s != far) | (k != last)))
        def _():
            for b in range(nblk):
                out_copy(k, b).wait_send()

        return carry

    lax.fori_loop(0, nseg, drain, 0)

    @pl.when(s == far)
    def _():
        for b in range(nblk):
            far_copy(b).wait_send()

    @pl.when(s == last)
    def _():
        for i in range(LS):
            ex_copy(LS * nseg + i, i).wait_send()
        for b in range(nblk):
            out_extra(b).wait()

    for b in range(nblk):
        out_local(s, b).wait()
    for dy in range(1, nseg):
        from_seg = (s + nseg - dy) % nseg

        @pl.when((s != last) | (from_seg != far))
        def _():
            for b in range(nblk):
                part = pl.ds(b * tile, tile)
                remote(
                    hsec.at[0, part],
                    out.at[0, from_seg, part],
                    o_send.at[0, b],
                    o_recv.at[dy, b],
                    yid(dy),
                ).wait_recv()


def hbm(a):
    return pltpu.with_memory_space_constraint(a, pltpu.HBM)


def shards(nseg, ndom, xc, feat, wts, bias, gain, tiles, cols, counts, cross, rows):
    micro, nodes, width = feat.shape
    depth = wts.shape[1]
    nblk, nslot, tile = tiles.shape[0], tiles.shape[1], tiles.shape[2]
    bound = rows.shape[1]
    layers = LS * nseg
    cross = cross.reshape(LS, nodes, bound)
    dma = pltpu.SemaphoreType.DMA
    anyspec = pl.BlockSpec(memory_space=pltpu.HBM)
    return pl.pallas_call(
        functools.partial(body, nseg, ndom, xc),
        out_shape=jax.ShapeDtypeStruct((1, micro, nodes, width), BF16),
        in_specs=[anyspec] * 9,
        out_specs=pl.BlockSpec(memory_space=pl.ANY),
        scratch_shapes=[
            pltpu.SMEM(cols.shape, jnp.int32),
            pltpu.SMEM(counts.shape, jnp.int32),
            pltpu.VMEM((LS, width), F32),
            pltpu.VMEM((LS, width), F32),
            pltpu.VMEM((LS, bound), jnp.int32),
            pltpu.VMEM((layers, depth, width), BF16),
            pltpu.VMEM((layers, nodes, bound), BF16),
            pltpu.VMEM((layers, 8, width), F32),
            pltpu.VMEM((nseg + 3, nodes, width), BF16),
            pltpu.VMEM((nodes, width), BF16),
            pltpu.VMEM((nodes, width), BF16),
            pltpu.VMEM((nodes, nodes), BF16),
            pltpu.VMEM((nblk, nslot, tile, tile), BF16),
            pltpu.VMEM((layers + LS, bound, width), BF16),
            pltpu.VMEM((layers + LS, bound, width), BF16),
            pltpu.VMEM((nodes, width), F32),
            dma((9,)),
            dma((layers + LS,)),
            dma((layers + LS,)),
            dma((LS, nseg)),
            dma((layers,)),
            dma((LS, nseg)),
            dma((layers,)),
            dma((nseg,)),
            dma((nseg,)),
            dma((layers, xc)),
            dma((layers, xc)),
            dma((layers, xc)),
            dma((layers, xc)),
            dma((nseg, nblk)),
            dma((nseg, nblk)),
            dma((2 * nblk,)),
            dma((nblk,)),
            dma((nblk,)),
        ],
        compiler_params=pltpu.CompilerParams(
            collective_id=0, has_side_effects=True, vmem_limit_bytes=48 << 20
        ),
        name="relay",
    )(*(hbm(a) for a in (feat, wts, bias, gain, tiles, cols, counts, cross, rows)))


def solution(mesh):
    in_specs = (
        P(None, "dom", None),
        P("segment", None, None),
        P("segment", None),
        P("segment", None),
        P("dom", None, None, None),
        P("dom", None),
        P("dom"),
        P("segment", "dom", None, None),
        P("segment", "dom"),
    )
    out_specs = P("segment", None, "dom", None)
    nseg, ndom = mesh.shape["segment"], mesh.shape["dom"]
    xc = X_CHIPS if ndom >= 4 * X_CHIPS else 2
    return jax.shard_map(
        functools.partial(shards, nseg, ndom, xc),
        mesh=mesh,
        in_specs=in_specs,
        out_specs=out_specs,
        check_vma=False,
    )
```

```python
import functools

import jax
import jax.numpy as jnp
from jax import lax
from jax.experimental import pallas as pl
from jax.experimental.pallas import tpu as pltpu
from jax.sharding import PartitionSpec as P

LS = 2
X_CHIPS = 4
MESH = pl.DeviceIdType.MESH
F32 = jnp.float32
BF16 = jnp.bfloat16


def dot(a, b):
    return jnp.dot(a, b, preferred_element_type=F32)


def body(
    nseg,
    ndom,
    xc,
    feat,
    wts,
    bias_hbm,
    gain_hbm,
    tiles_hbm,
    cols_hbm,
    counts_hbm,
    cross_hbm,
    rows_hbm,
    out,
    cols,
    counts,
    bias,
    gain,
    rows,
    wbuf,
    cbuf,
    small,
    hsec,
    hmid,
    xb,
    adj,
    tiles,
    snd,
    rcv,
    zp,
    loc_sem,
    ex_send,
    ex_recv,
    y_send,
    y_recv,
    c_send,
    c_recv,
    s_send,
    s_recv,
    x_send,
    x_recv,
    sib_send,
    sib_recv,
    o_send,
    o_recv,
    o_loc,
    f_send,
    f_recv,
):
    s = lax.axis_index("segment")
    d = lax.axis_index("dom")
    core = d % 2
    xi = (d // 2) % xc
    base = d - (d % (2 * xc))
    sib = base + xi * 2 + (1 - core)
    anti = (d + ndom // 2) % ndom
    depth, width = wbuf.shape[1], wbuf.shape[2]
    nblk, nslot, tile = tiles_hbm.shape[0], tiles_hbm.shape[1], tiles_hbm.shape[2]
    nodes = nblk * tile
    bound = rows.shape[1]
    shard = depth // (2 * xc)
    mine = (xi * 2 + core) * shard

    def yid(dy):
        return ((s + dy) % nseg, d)

    def xid(dx):
        return (s, base + ((xi + dx) % xc) * 2 + core)

    load_h = pltpu.make_async_copy(feat.at[s], hsec.at[0], loc_sem.at[0])
    load_w = pltpu.make_async_copy(wts, wbuf.at[pl.ds(s * LS, LS)], loc_sem.at[1])
    load_c = pltpu.make_async_copy(cross_hbm, cbuf.at[pl.ds(s * LS, LS)], loc_sem.at[2])
    load_t = pltpu.make_async_copy(tiles_hbm, tiles, loc_sem.at[3])
    loads = [
        pltpu.make_async_copy(a, b, loc_sem.at[4 + i])
        for i, (a, b) in enumerate(
            (
                (bias_hbm, bias),
                (gain_hbm, gain),
                (rows_hbm, rows),
                (cols_hbm, cols),
                (counts_hbm, counts),
            )
        )
    ]
    for load in loads:
        load.start()
    load_t.start()
    load_h.start()
    load_w.start()
    load_c.start()

    for load in loads:
        load.wait()
    for i in range(LS):
        small[s * LS + i] = jnp.zeros((8, width), F32)
        small[s * LS + i, 0:1, :] = bias[i : i + 1, :]
        small[s * LS + i, 1:2, :] = gain[i : i + 1, :]
        small[s * LS + i, 2:3, 0:bound] = rows[i : i + 1, :].astype(F32)

    barrier = pltpu.get_barrier_semaphore()
    peers = [yid(dy) for dy in range(1, nseg)]
    peers += [xid(dx) for dx in range(1, xc)]
    peers += [(s, sib), (s, anti)]
    for peer in peers:
        pl.semaphore_signal(barrier, inc=1, device_id=peer, device_id_type=MESH)
    pl.semaphore_wait(barrier, len(peers))

    def remote(src, dst, send, recv, peer):
        return pltpu.make_async_remote_copy(
            src_ref=src,
            dst_ref=dst,
            send_sem=send,
            recv_sem=recv,
            device_id=peer,
            device_id_type=MESH,
        )

    def w_copy(i, l, dy):
        return remote(
            wts.at[i, pl.ds(mine, shard)],
            wbuf.at[l, pl.ds(mine, shard)],
            y_send.at[i, dy],
            y_recv.at[l],
            yid(dy),
        )

    def c_copy(i, l, dy):
        return remote(cross_hbm.at[i], cbuf.at[l], c_send.at[i, dy], c_recv.at[l], yid(dy))

    def s_copy(k, dy):
        part = small.at[pl.ds(k * LS, LS)]
        return remote(part, part, s_send.at[dy], s_recv.at[k], yid(dy))

    def x_copy(l, dx):
        part = wbuf.at[l, pl.ds(mine, shard)]
        return remote(part, part, x_send.at[l, dx], x_recv.at[l, dx], xid(dx))

    def x_from(l, dx):
        start = (((xi + xc - dx) % xc) * 2 + core) * shard
        return wbuf.at[l, pl.ds(start, shard)]

    def sib_copy(l, q):
        part = x_from(l, q)
        return remote(part, part, sib_send.at[l, q], sib_recv.at[l, q], (s, sib))

    order = sorted(range(1, nseg), key=lambda dy: min(dy, nseg - dy))

    def owner_sends(k):
        if isinstance(k, int) and k >= nseg:
            return

        @pl.when(s == k)
        def _():
            for i in range(LS):
                for dy in order:
                    w_copy(i, k * LS + i, dy).start()
                if i == 0:
                    for dy in order:
                        s_copy(k, dy).start()
            for i in range(LS):
                for dy in order:
                    c_copy(i, k * LS + i, dy).start()

    def spread(k, i):
        if isinstance(k, int) and k >= nseg:
            return

        @pl.when((s != k) & (k < nseg))
        def _():
            l = k * LS + i
            w_copy(i, l, 1).wait_recv()
            for dx in range(1, xc):
                x_copy(l, dx).start()
            sib_copy(l, 0).start()

    def share(k, i):
        if isinstance(k, int) and k >= nseg:
            return

        @pl.when((s != k) & (k < nseg))
        def _():
            l = k * LS + i
            for dx in range(1, xc):
                x_copy(l, dx).wait_recv()
                sib_copy(l, dx).start()

    def wait_weights(k, i):
        @pl.when(s != k)
        def _():
            l = k * LS + i
            for q in range(xc):
                sib_copy(l, q).wait_recv()
            c_copy(i, l, 1).wait_recv()

    def ex_copy(l, pos):
        peer = (s, sib) if pos == 0 else (s, anti)
        return remote(snd.at[l], rcv.at[l], ex_send.at[l], ex_recv.at[l], peer)

    last = nseg - 1
    far = (last + nseg // 2) % nseg

    def far_copy(b):
        part = pl.ds(b * tile, tile)
        return remote(
            hsec.at[last, part],
            hsec.at[nseg + 1, part],
            f_send.at[b],
            f_recv.at[b],
            (last, d),
        )

    def out_copy(k, b):
        dy = (k + nseg - s) % nseg
        part = pl.ds(b * tile, tile)
        return remote(
            hsec.at[k + 1, part],
            out.at[0, s, part],
            o_send.at[k, b],
            o_recv.at[dy, b],
            (k, d),
        )

    def out_local(k, b):
        part = pl.ds(b * tile, tile)
        return pltpu.make_async_copy(hsec.at[k + 1, part], out.at[0, s, part], o_loc.at[b])

    def out_extra(b):
        part = pl.ds(b * tile, tile)
        return pltpu.make_async_copy(
            hsec.at[nseg + 2, part], out.at[0, far, part], o_loc.at[nblk + b]
        )

    owner_sends(0)

    load_t.wait()
    for r in range(nblk):
        for c in range(nblk):
            acc = jnp.zeros((tile, tile), F32)
            for k in range(nslot):
                live = (cols[r, k] == c) & (counts[r] > k)
                acc = acc + jnp.where(live, tiles[r, k].astype(F32), F32(0.0))
            adj[r * tile : (r + 1) * tile, c * tile : (c + 1) * tile] = acc.astype(BF16)
    load_h.wait()
    load_w.wait()
    load_c.wait()

    spread(0, 0)
    owner_sends(1)
    spread(0, 1)
    share(0, 0)
    owner_sends(2)

    def send_out(k, b):
        @pl.when(s == k)
        def _():
            out_local(k, b).start()

        @pl.when(s != k)
        def _():
            out_copy(k, b).start()

        @pl.when((s == far) & (k == last - 1))
        def _():
            far_copy(b).start()

    def layer(k, pos, src, dst, extra=False):
        l = k * LS + pos
        slot = LS * nseg + pos if extra else l
        gain_row = small[l, 1:2, :]
        bias_row = small[l, 0:1, :]
        for r in range(0, nodes, 64):
            hf = src[r : r + 64, :].astype(F32)
            ms = jnp.mean(hf * hf, axis=-1, keepdims=True)
            xb[r : r + 64, :] = (hf * lax.rsqrt(ms + 1e-5) * gain_row).astype(BF16)
        listed = jnp.broadcast_to(small[l, 2:3, 0:bound], (bound, bound)).T
        lane = lax.broadcasted_iota(jnp.int32, (bound, bound), 1).astype(F32)
        sent = jnp.zeros((bound, width), F32)
        for c in range(0, nodes, bound):
            pick = jnp.where(listed == lane + F32(c), F32(1.0), F32(0.0)).astype(BF16)
            sent = sent + dot(pick, xb[c : c + bound, :])
        snd[slot] = sent.astype(BF16)
        ex_copy(slot, pos).start()
        if not extra:
            wait_weights(k, pos)
        for r in range(0, nodes, tile):
            t = dot(adj[r : r + tile, :], xb[...]).astype(BF16)
            z = dot(xb[r : r + tile, :], wbuf[l, 0:width, :])
            zp[r : r + tile, :] = z + dot(t, wbuf[l, width:depth, :]) + bias_row
        if not extra:
            spread(k + 1, pos)
            if pos < LS - 1:
                share(k, pos + 1)
            else:
                share(k + 1, 0)
        ex_copy(slot, pos).wait_recv()
        y = dot(rcv[slot], wbuf[l, width:depth, :]).astype(BF16)
        for r in range(0, nodes, tile):
            z = zp[r : r + tile, :] + dot(cbuf[l, r : r + tile, :], y)
            half = z * F32(0.5)
            gate = half + half * jnp.tanh(half)
            dst[r : r + tile, :] = (src[r : r + tile, :].astype(F32) + gate).astype(BF16)
            if extra and pos == LS - 1:
                out_extra(r // tile).start()
            elif pos == LS - 1:
                send_out(k, r // tile)

    def section(k, carry):
        @pl.when(s != k)
        def _():
            s_copy(k, 1).wait_recv()

        layer(k, 0, hsec.at[k], hmid)
        owner_sends(k + 3)
        layer(k, 1, hmid, hsec.at[k + 1])
        return carry

    lax.fori_loop(0, last, section, 0)

    @pl.when(s == far)
    def _():
        s_copy(last, 1).wait_recv()
        wait_weights(last, 0)
        share(last, 1)
        wait_weights(last, 1)

    @pl.when(s != far)
    def _():
        section(last, 0)

    @pl.when(s == last)
    def _():
        for b in range(nblk):
            far_copy(b).wait_recv()
        layer(last, 0, hsec.at[nseg + 1], hmid, extra=True)
        layer(last, 1, hmid, hsec.at[nseg + 2], extra=True)

    for i in range(LS):
        for dy in range(1, nseg):
            w_copy(i, s * LS + i, dy).wait_send()
            c_copy(i, s * LS + i, dy).wait_send()
    for dy in range(1, nseg):
        s_copy(s, dy).wait_send()

    def drain(k, carry):
        for i in range(LS):
            l = k * LS + i

            @pl.when((s != far) | (k != last))
            def _():
                ex_copy(l, i).wait_send()

            @pl.when(s != k)
            def _():
                for q in range(xc):
                    sib_copy(l, q).wait_send()
                for dx in range(1, xc):
                    x_copy(l, dx).wait_send()

        @pl.when((s != k) & ((s != far) | (k != last)))
        def _():
            for b in range(nblk):
                out_copy(k, b).wait_send()

        return carry

    lax.fori_loop(0, nseg, drain, 0)

    @pl.when(s == far)
    def _():
        for b in range(nblk):
            far_copy(b).wait_send()

    @pl.when(s == last)
    def _():
        for i in range(LS):
            ex_copy(LS * nseg + i, i).wait_send()
        for b in range(nblk):
            out_extra(b).wait()

    for b in range(nblk):
        out_local(s, b).wait()
    for dy in range(1, nseg):
        from_seg = (s + nseg - dy) % nseg

        @pl.when((s != last) | (from_seg != far))
        def _():
            for b in range(nblk):
                part = pl.ds(b * tile, tile)
                remote(
                    hsec.at[0, part],
                    out.at[0, from_seg, part],
                    o_send.at[0, b],
                    o_recv.at[dy, b],
                    yid(dy),
                ).wait_recv()


def hbm(a):
    return pltpu.with_memory_space_constraint(a, pltpu.HBM)


def shards(nseg, ndom, xc, feat, wts, bias, gain, tiles, cols, counts, cross, rows):
    micro, nodes, width = feat.shape
    depth = wts.shape[1]
    nblk, nslot, tile = tiles.shape[0], tiles.shape[1], tiles.shape[2]
    bound = rows.shape[1]
    layers = LS * nseg
    cross = cross.reshape(LS, nodes, bound)
    dma = pltpu.SemaphoreType.DMA
    anyspec = pl.BlockSpec(memory_space=pltpu.HBM)
    return pl.pallas_call(
        functools.partial(body, nseg, ndom, xc),
        out_shape=jax.ShapeDtypeStruct((1, micro, nodes, width), BF16),
        in_specs=[anyspec] * 9,
        out_specs=pl.BlockSpec(memory_space=pl.ANY),
        scratch_shapes=[
            pltpu.SMEM(cols.shape, jnp.int32),
            pltpu.SMEM(counts.shape, jnp.int32),
            pltpu.VMEM((LS, width), F32),
            pltpu.VMEM((LS, width), F32),
            pltpu.VMEM((LS, bound), jnp.int32),
            pltpu.VMEM((layers, depth, width), BF16),
            pltpu.VMEM((layers, nodes, bound), BF16),
            pltpu.VMEM((layers, 8, width), F32),
            pltpu.VMEM((nseg + 3, nodes, width), BF16),
            pltpu.VMEM((nodes, width), BF16),
            pltpu.VMEM((nodes, width), BF16),
            pltpu.VMEM((nodes, nodes), BF16),
            pltpu.VMEM((nblk, nslot, tile, tile), BF16),
            pltpu.VMEM((layers + LS, bound, width), BF16),
            pltpu.VMEM((layers + LS, bound, width), BF16),
            pltpu.VMEM((nodes, width), F32),
            dma((9,)),
            dma((layers + LS,)),
            dma((layers + LS,)),
            dma((LS, nseg)),
            dma((layers,)),
            dma((LS, nseg)),
            dma((layers,)),
            dma((nseg,)),
            dma((nseg,)),
            dma((layers, xc)),
            dma((layers, xc)),
            dma((layers, xc)),
            dma((layers, xc)),
            dma((nseg, nblk)),
            dma((nseg, nblk)),
            dma((2 * nblk,)),
            dma((nblk,)),
            dma((nblk,)),
        ],
        compiler_params=pltpu.CompilerParams(
            collective_id=0, has_side_effects=True, vmem_limit_bytes=48 << 20
        ),
        name="relay",
    )(*(hbm(a) for a in (feat, wts, bias, gain, tiles, cols, counts, cross, rows)))


def solution(mesh):
    in_specs = (
        P(None, "dom", None),
        P("segment", None, None),
        P("segment", None),
        P("segment", None),
        P("dom", None, None, None),
        P("dom", None),
        P("dom"),
        P("segment", "dom", None, None),
        P("segment", "dom"),
    )
    out_specs = P("segment", None, "dom", None)
    nseg, ndom = mesh.shape["segment"], mesh.shape["dom"]
    xc = X_CHIPS if ndom >= 4 * X_CHIPS else 2
    return jax.shard_map(
        functools.partial(shards, nseg, ndom, xc),
        mesh=mesh,
        in_specs=in_specs,
        out_specs=out_specs,
        check_vma=False,
    )
```

```python
import functools

import jax
import jax.numpy as jnp
from jax import lax
from jax.experimental import pallas as pl
from jax.experimental.pallas import tpu as pltpu
from jax.sharding import PartitionSpec as P

LS = 2
X_CHIPS = 4
MESH = pl.DeviceIdType.MESH
F32 = jnp.float32
BF16 = jnp.bfloat16


def dot(a, b):
    return jnp.dot(a, b, preferred_element_type=F32)


def body(
    nseg,
    ndom,
    xc,
    feat,
    wts,
    bias_hbm,
    gain_hbm,
    tiles_hbm,
    cols_hbm,
    counts_hbm,
    cross_hbm,
    rows_hbm,
    out,
    cols,
    counts,
    bias,
    gain,
    rows,
    wbuf,
    cbuf,
    small,
    hsec,
    hmid,
    xb,
    adj,
    tiles,
    snd,
    rcv,
    zp,
    tb,
    picks,
    loc_sem,
    ex_send,
    ex_recv,
    y_send,
    y_recv,
    c_send,
    c_recv,
    s_send,
    s_recv,
    x_send,
    x_recv,
    sib_send,
    sib_recv,
    o_send,
    o_recv,
    o_loc,
    f_send,
    f_recv,
):
    s = lax.axis_index("segment")
    d = lax.axis_index("dom")
    core = d % 2
    xi = (d // 2) % xc
    base = d - (d % (2 * xc))
    sib = base + xi * 2 + (1 - core)
    anti = (d + ndom // 2) % ndom
    depth, width = wbuf.shape[1], wbuf.shape[2]
    nblk, nslot, tile = tiles_hbm.shape[0], tiles_hbm.shape[1], tiles_hbm.shape[2]
    nodes = nblk * tile
    bound = rows.shape[1]
    shard = depth // (2 * xc)
    mine = (xi * 2 + core) * shard
    halves = 2
    half_shard = shard // halves
    rstep, nstep = min(256, nodes), min(256, width)

    def yid(dy):
        return ((s + dy) % nseg, d)

    def xid(dx):
        return (s, base + ((xi + dx) % xc) * 2 + core)

    barrier = pltpu.get_barrier_semaphore()
    peers = [yid(dy) for dy in range(1, nseg)]
    peers += [xid(dx) for dx in range(1, xc)]
    peers += [(s, sib), (s, anti)]
    for peer in peers:
        pl.semaphore_signal(barrier, inc=1, device_id=peer, device_id_type=MESH)

    load_h = pltpu.make_async_copy(feat.at[s], hsec.at[0], loc_sem.at[0])
    load_w = pltpu.make_async_copy(wts, wbuf.at[pl.ds(s * LS, LS)], loc_sem.at[1])
    load_c = pltpu.make_async_copy(cross_hbm, cbuf.at[pl.ds(s * LS, LS)], loc_sem.at[2])
    load_t = pltpu.make_async_copy(tiles_hbm, tiles, loc_sem.at[3])
    loads = [
        pltpu.make_async_copy(a, b, loc_sem.at[4 + i])
        for i, (a, b) in enumerate(
            (
                (bias_hbm, bias),
                (gain_hbm, gain),
                (rows_hbm, rows),
                (cols_hbm, cols),
                (counts_hbm, counts),
            )
        )
    ]
    for load in loads:
        load.start()
    load_t.start()
    load_h.start()
    load_w.start()
    load_c.start()

    for load in loads:
        load.wait()
    for i in range(LS):
        small[s * LS + i] = jnp.zeros((8, width), F32)
        small[s * LS + i, 0:1, :] = bias[i : i + 1, :]
        small[s * LS + i, 1:2, :] = gain[i : i + 1, :]
        small[s * LS + i, 2:3, 0:bound] = rows[i : i + 1, :].astype(F32)

    pl.semaphore_wait(barrier, len(peers))

    def remote(src, dst, send, recv, peer):
        return pltpu.make_async_remote_copy(
            src_ref=src,
            dst_ref=dst,
            send_sem=send,
            recv_sem=recv,
            device_id=peer,
            device_id_type=MESH,
        )

    def w_copy(i, l, dy, h):
        part = pl.ds(mine + h * half_shard, half_shard)
        return remote(
            wts.at[i, part],
            wbuf.at[l, part],
            y_send.at[i, dy, h],
            y_recv.at[l, h],
            yid(dy),
        )

    def c_copy(i, l, dy):
        return remote(cross_hbm.at[i], cbuf.at[l], c_send.at[i, dy], c_recv.at[l], yid(dy))

    def s_copy(k, dy):
        part = small.at[pl.ds(k * LS, LS)]
        return remote(part, part, s_send.at[dy], s_recv.at[k], yid(dy))

    def x_copy(l, dx, h):
        part = wbuf.at[l, pl.ds(mine + h * half_shard, half_shard)]
        return remote(part, part, x_send.at[l, dx, h], x_recv.at[l, dx, h], xid(dx))

    def x_from(l, dx):
        start = (((xi + xc - dx) % xc) * 2 + core) * shard
        return wbuf.at[l, pl.ds(start, shard)]

    def sib_copy(l, q):
        part = x_from(l, q)
        return remote(part, part, sib_send.at[l, q], sib_recv.at[l, q], (s, sib))

    order = sorted(range(1, nseg), key=lambda dy: min(dy, nseg - dy))

    def owner_sends(k):
        if isinstance(k, int) and k >= nseg:
            return

        @pl.when(s == k)
        def _():
            for i in range(LS):
                for h in range(halves):
                    for dy in order:
                        w_copy(i, k * LS + i, dy, h).start()
                if i == 0:
                    for dy in order:
                        s_copy(k, dy).start()
            for i in range(LS):
                for dy in order:
                    c_copy(i, k * LS + i, dy).start()

    def spread(k, i):
        if isinstance(k, int) and k >= nseg:
            return

        @pl.when((s != k) & (k < nseg))
        def _():
            l = k * LS + i
            for h in range(halves):
                w_copy(i, l, 1, h).wait_recv()
                for dx in range(1, xc):
                    x_copy(l, dx, h).start()
            sib_copy(l, 0).start()

    def share(k, i):
        if isinstance(k, int) and k >= nseg:
            return

        @pl.when((s != k) & (k < nseg))
        def _():
            l = k * LS + i
            for dx in range(1, xc):
                for h in range(halves):
                    x_copy(l, dx, h).wait_recv()
                sib_copy(l, dx).start()

    def wait_weights(k, i):
        @pl.when(s != k)
        def _():
            l = k * LS + i
            for q in range(xc):
                sib_copy(l, q).wait_recv()
            c_copy(i, l, 1).wait_recv()

    def ex_copy(l, pos):
        peer = (s, sib) if pos == 0 else (s, anti)
        return remote(snd.at[l], rcv.at[l], ex_send.at[l], ex_recv.at[l], peer)

    last = nseg - 1
    far = (last + nseg // 2) % nseg

    def far_copy(b):
        part = pl.ds(b * tile, tile)
        return remote(
            hsec.at[last, part],
            hsec.at[nseg + 1, part],
            f_send.at[b],
            f_recv.at[b],
            (last, d),
        )

    def out_copy(k, b):
        dy = (k + nseg - s) % nseg
        part = pl.ds(b * tile, tile)
        return remote(
            hsec.at[k + 1, part],
            out.at[0, s, part],
            o_send.at[k, b],
            o_recv.at[dy, b],
            (k, d),
        )

    def out_local(k, b):
        part = pl.ds(b * tile, tile)
        return pltpu.make_async_copy(hsec.at[k + 1, part], out.at[0, s, part], o_loc.at[b])

    def out_extra(b):
        part = pl.ds(b * tile, tile)
        return pltpu.make_async_copy(
            hsec.at[nseg + 2, part], out.at[0, far, part], o_loc.at[nblk + b]
        )

    owner_sends(0)

    load_t.wait()
    for r in range(nblk):
        for c in range(nblk):
            acc = jnp.zeros((tile, tile), F32)
            for k in range(nslot):
                live = (cols[r, k] == c) & (counts[r] > k)
                acc = acc + jnp.where(live, tiles[r, k].astype(F32), F32(0.0))
            adj[r * tile : (r + 1) * tile, c * tile : (c + 1) * tile] = acc.astype(BF16)
    load_h.wait()
    load_w.wait()
    load_c.wait()


    def send_out(k, b):
        @pl.when(s == k)
        def _():
            out_local(k, b).start()

        @pl.when(s != k)
        def _():
            out_copy(k, b).start()

        @pl.when((s == far) & (k == last - 1))
        def _():
            far_copy(b).start()

    def norm(hf, gain_row):
        ms = jnp.mean(hf * hf, axis=-1, keepdims=True)
        return (hf * lax.rsqrt(ms + 1e-5) * gain_row).astype(BF16)

    def make_x(src, l):
        gain_row = small[l, 1:2, :]
        for r in range(0, nodes, 64):
            xb[r : r + 64, :] = norm(src[r : r + 64, :].astype(F32), gain_row)

    def make_pick(l, pos):
        listed = jnp.broadcast_to(small[l, 2:3, 0:bound], (bound, bound)).T
        lane = lax.broadcasted_iota(jnp.int32, (bound, bound), 1).astype(F32)
        for c in range(0, nodes, bound):
            hit = jnp.where(listed == lane + F32(c), F32(1.0), F32(0.0))
            picks[pos, :, c : c + bound] = hit.astype(BF16)

    def layer(k, pos, src, dst, extra=False):
        l = k * LS + pos
        slot = LS * nseg + pos if extra else l
        final = isinstance(k, int) and k == last
        follow = pos < LS - 1 or not final
        snd[slot] = dot(picks[pos], xb[...]).astype(BF16)
        ex_copy(slot, pos).start()
        for r in range(0, nodes, rstep):
            tb[r : r + rstep, :] = dot(adj[r : r + rstep, :], xb[...]).astype(BF16)
        if not extra:
            wait_weights(k, pos)
        bias_row = small[l, 0:1, :]
        for n in range(0, width, nstep):
            for r in range(0, nodes, rstep):
                z = dot(xb[r : r + rstep, :], wbuf[l, 0:width, n : n + nstep])
                z = z + dot(tb[r : r + rstep, :], wbuf[l, width:depth, n : n + nstep])
                zp[r : r + rstep, n : n + nstep] = z + bias_row[:, n : n + nstep]
        if not extra:
            spread(k + 1, pos)
            if pos < LS - 1:
                share(k, pos + 1)
                make_pick(l + 1, pos + 1)
            else:
                share(k + 1, 0)
                if follow:

                    @pl.when(s != k + 1)
                    def _():
                        s_copy(k + 1, 1).wait_recv()

                    make_pick(l + 1, 0)
        ex_copy(slot, pos).wait_recv()
        y = dot(rcv[slot], wbuf[l, width:depth, :]).astype(BF16)
        for r in range(0, nodes, tile):
            z = zp[r : r + tile, :] + dot(cbuf[l, r : r + tile, :], y)
            half = z * F32(0.5)
            gate = half + half * jnp.tanh(half)
            hb = (src[r : r + tile, :].astype(F32) + gate).astype(BF16)
            dst[r : r + tile, :] = hb
            if follow:
                xb[r : r + tile, :] = norm(hb.astype(F32), small[l + 1, 1:2, :])
            if extra and pos == LS - 1:
                out_extra(r // tile).start()
            elif pos == LS - 1:
                send_out(k, r // tile)

    def section(k, carry):
        layer(k, 0, hsec.at[k], hmid)
        owner_sends(k + 3)
        layer(k, 1, hmid, hsec.at[k + 1])
        return carry

    spread(0, 0)
    owner_sends(1)

    @pl.when(s != 0)
    def _():
        s_copy(0, 1).wait_recv()

    make_x(hsec.at[0], 0)
    make_pick(0, 0)
    spread(0, 1)
    share(0, 0)
    owner_sends(2)

    lax.fori_loop(0, last, section, 0)

    @pl.when(s == far)
    def _():
        wait_weights(last, 0)
        share(last, 1)
        wait_weights(last, 1)

    @pl.when(s != far)
    def _():
        section(last, 0)

    @pl.when(s == last)
    def _():
        for b in range(nblk):
            far_copy(b).wait_recv()
        make_x(hsec.at[nseg + 1], last * LS)
        layer(last, 0, hsec.at[nseg + 1], hmid, extra=True)
        layer(last, 1, hmid, hsec.at[nseg + 2], extra=True)

    for i in range(LS):
        for dy in range(1, nseg):
            for h in range(halves):
                w_copy(i, s * LS + i, dy, h).wait_send()
            c_copy(i, s * LS + i, dy).wait_send()
    for dy in range(1, nseg):
        s_copy(s, dy).wait_send()

    def drain(k, carry):
        for i in range(LS):
            l = k * LS + i

            @pl.when((s != far) | (k != last))
            def _():
                ex_copy(l, i).wait_send()

            @pl.when(s != k)
            def _():
                for q in range(xc):
                    sib_copy(l, q).wait_send()
                for dx in range(1, xc):
                    for h in range(halves):
                        x_copy(l, dx, h).wait_send()

        @pl.when((s != k) & ((s != far) | (k != last)))
        def _():
            for b in range(nblk):
                out_copy(k, b).wait_send()

        return carry

    lax.fori_loop(0, nseg, drain, 0)

    @pl.when(s == far)
    def _():
        for b in range(nblk):
            far_copy(b).wait_send()

    @pl.when(s == last)
    def _():
        for i in range(LS):
            ex_copy(LS * nseg + i, i).wait_send()
        for b in range(nblk):
            out_extra(b).wait()

    for b in range(nblk):
        out_local(s, b).wait()
    for dy in range(1, nseg):
        from_seg = (s + nseg - dy) % nseg

        @pl.when((s != last) | (from_seg != far))
        def _():
            for b in range(nblk):
                part = pl.ds(b * tile, tile)
                remote(
                    hsec.at[0, part],
                    out.at[0, from_seg, part],
                    o_send.at[0, b],
                    o_recv.at[dy, b],
                    yid(dy),
                ).wait_recv()


def hbm(a):
    return pltpu.with_memory_space_constraint(a, pltpu.HBM)


def shards(nseg, ndom, xc, feat, wts, bias, gain, tiles, cols, counts, cross, rows):
    micro, nodes, width = feat.shape
    depth = wts.shape[1]
    nblk, nslot, tile = tiles.shape[0], tiles.shape[1], tiles.shape[2]
    bound = rows.shape[1]
    layers = LS * nseg
    cross = cross.reshape(LS, nodes, bound)
    dma = pltpu.SemaphoreType.DMA
    anyspec = pl.BlockSpec(memory_space=pltpu.HBM)
    return pl.pallas_call(
        functools.partial(body, nseg, ndom, xc),
        out_shape=jax.ShapeDtypeStruct((1, micro, nodes, width), BF16),
        in_specs=[anyspec] * 9,
        out_specs=pl.BlockSpec(memory_space=pl.ANY),
        scratch_shapes=[
            pltpu.SMEM(cols.shape, jnp.int32),
            pltpu.SMEM(counts.shape, jnp.int32),
            pltpu.VMEM((LS, width), F32),
            pltpu.VMEM((LS, width), F32),
            pltpu.VMEM((LS, bound), jnp.int32),
            pltpu.VMEM((layers, depth, width), BF16),
            pltpu.VMEM((layers, nodes, bound), BF16),
            pltpu.VMEM((layers, 8, width), F32),
            pltpu.VMEM((nseg + 3, nodes, width), BF16),
            pltpu.VMEM((nodes, width), BF16),
            pltpu.VMEM((nodes, width), BF16),
            pltpu.VMEM((nodes, nodes), BF16),
            pltpu.VMEM((nblk, nslot, tile, tile), BF16),
            pltpu.VMEM((layers + LS, bound, width), BF16),
            pltpu.VMEM((layers + LS, bound, width), BF16),
            pltpu.VMEM((nodes, width), F32),
            pltpu.VMEM((nodes, width), BF16),
            pltpu.VMEM((LS, bound, nodes), BF16),
            dma((9,)),
            dma((layers + LS,)),
            dma((layers + LS,)),
            dma((LS, nseg, 2)),
            dma((layers, 2)),
            dma((LS, nseg)),
            dma((layers,)),
            dma((nseg,)),
            dma((nseg,)),
            dma((layers, xc, 2)),
            dma((layers, xc, 2)),
            dma((layers, xc)),
            dma((layers, xc)),
            dma((nseg, nblk)),
            dma((nseg, nblk)),
            dma((2 * nblk,)),
            dma((nblk,)),
            dma((nblk,)),
        ],
        compiler_params=pltpu.CompilerParams(
            collective_id=0, has_side_effects=True, vmem_limit_bytes=48 << 20
        ),
        name="relay",
    )(*(hbm(a) for a in (feat, wts, bias, gain, tiles, cols, counts, cross, rows)))


def solution(mesh):
    in_specs = (
        P(None, "dom", None),
        P("segment", None, None),
        P("segment", None),
        P("segment", None),
        P("dom", None, None, None),
        P("dom", None),
        P("dom"),
        P("segment", "dom", None, None),
        P("segment", "dom"),
    )
    out_specs = P("segment", None, "dom", None)
    nseg, ndom = mesh.shape["segment"], mesh.shape["dom"]
    xc = X_CHIPS if ndom >= 4 * X_CHIPS else 2
    return jax.shard_map(
        functools.partial(shards, nseg, ndom, xc),
        mesh=mesh,
        in_specs=in_specs,
        out_specs=out_specs,
        check_vma=False,
    )
```

```python
import functools

import jax
import jax.numpy as jnp
from jax import lax
from jax.experimental import pallas as pl
from jax.experimental.pallas import tpu as pltpu
from jax.sharding import PartitionSpec as P

LS = 2
X_CHIPS = 4
MESH = pl.DeviceIdType.MESH
F32 = jnp.float32
BF16 = jnp.bfloat16


def dot(a, b):
    return jnp.dot(a, b, preferred_element_type=F32)


def body(
    nseg,
    ndom,
    xc,
    feat,
    wts,
    bias_hbm,
    gain_hbm,
    tiles_hbm,
    cols_hbm,
    counts_hbm,
    cross_hbm,
    rows_hbm,
    out,
    cols,
    counts,
    bias,
    gain,
    rows,
    wbuf,
    cbuf,
    small,
    hsec,
    hmid,
    xb,
    adj,
    tiles,
    snd,
    rcv,
    zp,
    tb,
    picks,
    loc_sem,
    ex_send,
    ex_recv,
    y_send,
    y_recv,
    c_send,
    c_recv,
    s_send,
    s_recv,
    x_send,
    x_recv,
    sib_send,
    sib_recv,
    o_send,
    o_recv,
    o_loc,
    f_send,
    f_recv,
):
    s = lax.axis_index("segment")
    d = lax.axis_index("dom")
    core = d % 2
    xi = (d // 2) % xc
    base = d - (d % (2 * xc))
    sib = base + xi * 2 + (1 - core)
    anti = (d + ndom // 2) % ndom
    depth, width = wbuf.shape[1], wbuf.shape[2]
    nblk, nslot, tile = tiles_hbm.shape[0], tiles_hbm.shape[1], tiles_hbm.shape[2]
    nodes = nblk * tile
    bound = rows.shape[1]
    shard = depth // (2 * xc)
    mine = (xi * 2 + core) * shard
    halves = 2
    half_shard = shard // halves
    rstep, nstep = min(256, nodes), min(256, width)

    def yid(dy):
        return ((s + dy) % nseg, d)

    def xid(dx):
        return (s, base + ((xi + dx) % xc) * 2 + core)

    barrier = pltpu.get_barrier_semaphore()
    peers = [yid(dy) for dy in range(1, nseg)]
    peers += [xid(dx) for dx in range(1, xc)]
    peers += [(s, sib), (s, anti)]
    for peer in peers:
        pl.semaphore_signal(barrier, inc=1, device_id=peer, device_id_type=MESH)

    load_h = pltpu.make_async_copy(feat.at[s], hsec.at[0], loc_sem.at[0])
    load_w = pltpu.make_async_copy(wts, wbuf.at[pl.ds(s * LS, LS)], loc_sem.at[1])
    load_c = pltpu.make_async_copy(cross_hbm, cbuf.at[pl.ds(s * LS, LS)], loc_sem.at[2])
    load_t = pltpu.make_async_copy(tiles_hbm, tiles, loc_sem.at[3])
    loads = [
        pltpu.make_async_copy(a, b, loc_sem.at[4 + i])
        for i, (a, b) in enumerate(
            (
                (bias_hbm, bias),
                (gain_hbm, gain),
                (rows_hbm, rows),
                (cols_hbm, cols),
                (counts_hbm, counts),
            )
        )
    ]
    for load in loads:
        load.start()
    load_t.start()
    load_h.start()
    load_w.start()
    load_c.start()

    for load in loads:
        load.wait()
    for i in range(LS):
        small[s * LS + i] = jnp.zeros((8, width), F32)
        small[s * LS + i, 0:1, :] = bias[i : i + 1, :]
        small[s * LS + i, 1:2, :] = gain[i : i + 1, :]
        small[s * LS + i, 2:3, 0:bound] = rows[i : i + 1, :].astype(F32)

    pl.semaphore_wait(barrier, len(peers))

    def remote(src, dst, send, recv, peer):
        return pltpu.make_async_remote_copy(
            src_ref=src,
            dst_ref=dst,
            send_sem=send,
            recv_sem=recv,
            device_id=peer,
            device_id_type=MESH,
        )

    def w_copy(i, l, dy, h):
        part = pl.ds(mine + h * half_shard, half_shard)
        return remote(
            wts.at[i, part],
            wbuf.at[l, part],
            y_send.at[i, dy, h],
            y_recv.at[l, h],
            yid(dy),
        )

    def c_copy(i, l, dy):
        return remote(cross_hbm.at[i], cbuf.at[l], c_send.at[i, dy], c_recv.at[l], yid(dy))

    def s_copy(k, dy):
        part = small.at[pl.ds(k * LS, LS)]
        return remote(part, part, s_send.at[dy], s_recv.at[k], yid(dy))

    def x_copy(l, dx, h):
        part = wbuf.at[l, pl.ds(mine + h * half_shard, half_shard)]
        return remote(part, part, x_send.at[l, dx, h], x_recv.at[l, dx, h], xid(dx))

    def x_from(l, dx):
        start = (((xi + xc - dx) % xc) * 2 + core) * shard
        return wbuf.at[l, pl.ds(start, shard)]

    def sib_copy(l, q):
        part = x_from(l, q)
        return remote(part, part, sib_send.at[l, q], sib_recv.at[l, q], (s, sib))

    order = sorted(range(1, nseg), key=lambda dy: min(dy, nseg - dy))

    def owner_sends(k):
        if isinstance(k, int) and k >= nseg:
            return

        @pl.when(s == k)
        def _():
            for i in range(LS):
                first = order[::-1] if isinstance(k, int) and k == 0 else order
                for h in range(halves):
                    for dy in first:
                        w_copy(i, k * LS + i, dy, h).start()
                if i == 0:
                    for dy in order:
                        s_copy(k, dy).start()
            for i in range(LS):
                for dy in order:
                    c_copy(i, k * LS + i, dy).start()

    def spread(k, i):
        if isinstance(k, int) and k >= nseg:
            return

        @pl.when((s != k) & (k < nseg))
        def _():
            l = k * LS + i
            for h in range(halves):
                w_copy(i, l, 1, h).wait_recv()
                for dx in range(1, xc):
                    x_copy(l, dx, h).start()
            sib_copy(l, 0).start()

    def share(k, i):
        if isinstance(k, int) and k >= nseg:
            return

        @pl.when((s != k) & (k < nseg))
        def _():
            l = k * LS + i
            for dx in range(1, xc):
                for h in range(halves):
                    x_copy(l, dx, h).wait_recv()
                sib_copy(l, dx).start()

    def wait_weights(k, i):
        @pl.when(s != k)
        def _():
            l = k * LS + i
            for q in range(xc):
                sib_copy(l, q).wait_recv()
            c_copy(i, l, 1).wait_recv()

    def ex_copy(l, pos):
        peer = (s, sib) if pos == 0 else (s, anti)
        return remote(snd.at[l], rcv.at[l], ex_send.at[l], ex_recv.at[l], peer)

    last = nseg - 1
    far = (last + nseg // 2) % nseg

    def far_copy(b):
        part = pl.ds(b * tile, tile)
        return remote(
            hsec.at[last, part],
            hsec.at[nseg + 1, part],
            f_send.at[b],
            f_recv.at[b],
            (last, d),
        )

    def out_copy(k, b):
        dy = (k + nseg - s) % nseg
        part = pl.ds(b * tile, tile)
        return remote(
            hsec.at[k + 1, part],
            out.at[0, s, part],
            o_send.at[k, b],
            o_recv.at[dy, b],
            (k, d),
        )

    def out_local(k, b):
        part = pl.ds(b * tile, tile)
        return pltpu.make_async_copy(hsec.at[k + 1, part], out.at[0, s, part], o_loc.at[b])

    def out_extra(b):
        part = pl.ds(b * tile, tile)
        return pltpu.make_async_copy(
            hsec.at[nseg + 2, part], out.at[0, far, part], o_loc.at[nblk + b]
        )

    owner_sends(0)

    load_t.wait()
    for r in range(nblk):
        for c in range(nblk):
            acc = jnp.zeros((tile, tile), F32)
            for k in range(nslot):
                live = (cols[r, k] == c) & (counts[r] > k)
                acc = acc + jnp.where(live, tiles[r, k].astype(F32), F32(0.0))
            adj[r * tile : (r + 1) * tile, c * tile : (c + 1) * tile] = acc.astype(BF16)
    load_h.wait()
    load_w.wait()
    load_c.wait()


    def send_out(k, b):
        @pl.when(s == k)
        def _():
            out_local(k, b).start()

        @pl.when(s != k)
        def _():
            out_copy(k, b).start()

        @pl.when((s == far) & (k == last - 1))
        def _():
            far_copy(b).start()

    def norm(hf, gain_row):
        ms = jnp.mean(hf * hf, axis=-1, keepdims=True)
        return (hf * lax.rsqrt(ms + 1e-5) * gain_row).astype(BF16)

    def make_x(src, l):
        gain_row = small[l, 1:2, :]
        for r in range(0, nodes, 64):
            xb[r : r + 64, :] = norm(src[r : r + 64, :].astype(F32), gain_row)

    def make_pick(l, pos):
        listed = jnp.broadcast_to(small[l, 2:3, 0:bound], (bound, bound)).T
        lane = lax.broadcasted_iota(jnp.int32, (bound, bound), 1).astype(F32)
        for c in range(0, nodes, bound):
            hit = jnp.where(listed == lane + F32(c), F32(1.0), F32(0.0))
            picks[pos, :, c : c + bound] = hit.astype(BF16)

    def layer(k, pos, src, dst, extra=False):
        l = k * LS + pos
        slot = LS * nseg + pos if extra else l
        final = isinstance(k, int) and k == last
        follow = pos < LS - 1 or not final
        snd[slot] = dot(picks[pos], xb[...]).astype(BF16)
        ex_copy(slot, pos).start()
        for r in range(0, nodes, rstep):
            tb[r : r + rstep, :] = dot(adj[r : r + rstep, :], xb[...]).astype(BF16)
        if not extra:
            wait_weights(k, pos)
        bias_row = small[l, 0:1, :]
        for n in range(0, width, nstep):
            for r in range(0, nodes, rstep):
                z = dot(xb[r : r + rstep, :], wbuf[l, 0:width, n : n + nstep])
                z = z + dot(tb[r : r + rstep, :], wbuf[l, width:depth, n : n + nstep])
                zp[r : r + rstep, n : n + nstep] = z + bias_row[:, n : n + nstep]
        if not extra:
            spread(k + 1, pos)
            if pos < LS - 1:
                share(k, pos + 1)
                make_pick(l + 1, pos + 1)
            else:
                share(k + 1, 0)
                if follow:

                    @pl.when(s != k + 1)
                    def _():
                        s_copy(k + 1, 1).wait_recv()

                    make_pick(l + 1, 0)
        ex_copy(slot, pos).wait_recv()
        y = dot(rcv[slot], wbuf[l, width:depth, :]).astype(BF16)
        for r in range(0, nodes, tile):
            z = zp[r : r + tile, :] + dot(cbuf[l, r : r + tile, :], y)
            half = z * F32(0.5)
            gate = half + half * jnp.tanh(half)
            hb = (src[r : r + tile, :].astype(F32) + gate).astype(BF16)
            dst[r : r + tile, :] = hb
            if follow:
                xb[r : r + tile, :] = norm(hb.astype(F32), small[l + 1, 1:2, :])
            if extra and pos == LS - 1:
                out_extra(r // tile).start()
            elif pos == LS - 1:
                send_out(k, r // tile)

    def section(k, carry):
        layer(k, 0, hsec.at[k], hmid)
        owner_sends(k + 3)
        layer(k, 1, hmid, hsec.at[k + 1])
        return carry

    spread(0, 0)
    owner_sends(1)

    @pl.when(s != 0)
    def _():
        s_copy(0, 1).wait_recv()

    make_x(hsec.at[0], 0)
    make_pick(0, 0)
    spread(0, 1)
    share(0, 0)
    owner_sends(2)

    lax.fori_loop(0, last, section, 0)

    @pl.when(s == far)
    def _():
        wait_weights(last, 0)
        share(last, 1)
        wait_weights(last, 1)

    @pl.when(s != far)
    def _():
        section(last, 0)

    @pl.when(s == last)
    def _():
        for b in range(nblk):
            far_copy(b).wait_recv()
        make_x(hsec.at[nseg + 1], last * LS)
        layer(last, 0, hsec.at[nseg + 1], hmid, extra=True)
        layer(last, 1, hmid, hsec.at[nseg + 2], extra=True)

    for i in range(LS):
        for dy in range(1, nseg):
            for h in range(halves):
                w_copy(i, s * LS + i, dy, h).wait_send()
            c_copy(i, s * LS + i, dy).wait_send()
    for dy in range(1, nseg):
        s_copy(s, dy).wait_send()

    def drain(k, carry):
        for i in range(LS):
            l = k * LS + i

            @pl.when((s != far) | (k != last))
            def _():
                ex_copy(l, i).wait_send()

            @pl.when(s != k)
            def _():
                for q in range(xc):
                    sib_copy(l, q).wait_send()
                for dx in range(1, xc):
                    for h in range(halves):
                        x_copy(l, dx, h).wait_send()

        @pl.when((s != k) & ((s != far) | (k != last)))
        def _():
            for b in range(nblk):
                out_copy(k, b).wait_send()

        return carry

    lax.fori_loop(0, nseg, drain, 0)

    @pl.when(s == far)
    def _():
        for b in range(nblk):
            far_copy(b).wait_send()

    @pl.when(s == last)
    def _():
        for i in range(LS):
            ex_copy(LS * nseg + i, i).wait_send()
        for b in range(nblk):
            out_extra(b).wait()

    for b in range(nblk):
        out_local(s, b).wait()
    for dy in range(1, nseg):
        from_seg = (s + nseg - dy) % nseg

        @pl.when((s != last) | (from_seg != far))
        def _():
            for b in range(nblk):
                part = pl.ds(b * tile, tile)
                remote(
                    hsec.at[0, part],
                    out.at[0, from_seg, part],
                    o_send.at[0, b],
                    o_recv.at[dy, b],
                    yid(dy),
                ).wait_recv()


def hbm(a):
    return pltpu.with_memory_space_constraint(a, pltpu.HBM)


def shards(nseg, ndom, xc, feat, wts, bias, gain, tiles, cols, counts, cross, rows):
    micro, nodes, width = feat.shape
    depth = wts.shape[1]
    nblk, nslot, tile = tiles.shape[0], tiles.shape[1], tiles.shape[2]
    bound = rows.shape[1]
    layers = LS * nseg
    cross = cross.reshape(LS, nodes, bound)
    dma = pltpu.SemaphoreType.DMA
    anyspec = pl.BlockSpec(memory_space=pltpu.HBM)
    return pl.pallas_call(
        functools.partial(body, nseg, ndom, xc),
        out_shape=jax.ShapeDtypeStruct((1, micro, nodes, width), BF16),
        in_specs=[anyspec] * 9,
        out_specs=pl.BlockSpec(memory_space=pl.ANY),
        scratch_shapes=[
            pltpu.SMEM(cols.shape, jnp.int32),
            pltpu.SMEM(counts.shape, jnp.int32),
            pltpu.VMEM((LS, width), F32),
            pltpu.VMEM((LS, width), F32),
            pltpu.VMEM((LS, bound), jnp.int32),
            pltpu.VMEM((layers, depth, width), BF16),
            pltpu.VMEM((layers, nodes, bound), BF16),
            pltpu.VMEM((layers, 8, width), F32),
            pltpu.VMEM((nseg + 3, nodes, width), BF16),
            pltpu.VMEM((nodes, width), BF16),
            pltpu.VMEM((nodes, width), BF16),
            pltpu.VMEM((nodes, nodes), BF16),
            pltpu.VMEM((nblk, nslot, tile, tile), BF16),
            pltpu.VMEM((layers + LS, bound, width), BF16),
            pltpu.VMEM((layers + LS, bound, width), BF16),
            pltpu.VMEM((nodes, width), F32),
            pltpu.VMEM((nodes, width), BF16),
            pltpu.VMEM((LS, bound, nodes), BF16),
            dma((9,)),
            dma((layers + LS,)),
            dma((layers + LS,)),
            dma((LS, nseg, 2)),
            dma((layers, 2)),
            dma((LS, nseg)),
            dma((layers,)),
            dma((nseg,)),
            dma((nseg,)),
            dma((layers, xc, 2)),
            dma((layers, xc, 2)),
            dma((layers, xc)),
            dma((layers, xc)),
            dma((nseg, nblk)),
            dma((nseg, nblk)),
            dma((2 * nblk,)),
            dma((nblk,)),
            dma((nblk,)),
        ],
        compiler_params=pltpu.CompilerParams(
            collective_id=0, has_side_effects=True, vmem_limit_bytes=48 << 20
        ),
        name="relay",
    )(*(hbm(a) for a in (feat, wts, bias, gain, tiles, cols, counts, cross, rows)))


def solution(mesh):
    in_specs = (
        P(None, "dom", None),
        P("segment", None, None),
        P("segment", None),
        P("segment", None),
        P("dom", None, None, None),
        P("dom", None),
        P("dom"),
        P("segment", "dom", None, None),
        P("segment", "dom"),
    )
    out_specs = P("segment", None, "dom", None)
    nseg, ndom = mesh.shape["segment"], mesh.shape["dom"]
    xc = X_CHIPS if ndom >= 4 * X_CHIPS else 2
    return jax.shard_map(
        functools.partial(shards, nseg, ndom, xc),
        mesh=mesh,
        in_specs=in_specs,
        out_specs=out_specs,
        check_vma=False,
    )
```
